128 devices in a mesh: comp: 16 (over y, x), space: 8 (over z, core).
Axes of the slice: x: 4, y: 4, z: 4, core: 2. Of those that a mesh axis runs over, the one named last changes fastest.
Arguments:
- spectrum: float32 [1296, 512, 256], P('comp', 'space'), may hold values from 0.05 to 2
- mask: int32 [512, 256], P('space'), may hold values 0 or 1
- depth_level: int32 [512, 256], P('space'), may hold values from 0 to 7
- speed_table: float32 [36, 8], replicated, may hold values from 0.2 to 1.8
- wind_u: float32 [512, 256], P('space'), may hold values from -4 to 4
- wind_v: float32 [512, 256], P('space'), may hold values from -4 to 4
- substeps: int32 [512], P('space'), may hold values from 1 to 4, as said below
- coupling: bfloat16 [1296, 1296], replicated, may hold values from -0.15625 to 0.15625
Outputs:
- spectrum_next: float32 [1296, 512, 256], P('comp', 'space')
The draws below stay inside these ranges and needn't reach their ends.
Inputs may be any that keep to these rules, and one draw needn't show every extreme that they name: `substeps`: every strip of 64 consecutive rows holds a run of 8 consecutive rows with 4 turns.
All inputs are finite; a program needn't handle non-finite values. No bound on the sum of `mask` on one device may be relied on, other than what follows from the above.
Results may differ from the reference program's by a relative error of at most 0.0011.
Values sent between devices are 32-bit elements; how exact they have to be, the bound alone decides.
No kernel may reach another device: no remote copies, remote signals or barrier semaphores. Data moves between devices by JAX's collectives and lax.ppermute only.
A program may use at most 128 MiB of HBM per device.

```python
import math
import jax
import jax.numpy as jnp
from jax import lax

NF = 36
ND = 36
LEVELS = 8
SUB_MOST = 4
ROWS_DEV = 4
NY = 256
NC = 1296
SX = 64
NX = 512


def draw_substeps(key, part):
    key_base, key_band = jax.random.split(jax.random.fold_in(key, 11))
    background = jax.random.randint(key_base, (NX,), 1, 3)
    strips = NX // SX
    band_start = jax.random.randint(key_band, (strips,), 0, SX - 2 * ROWS_DEV + 1)
    row_index = jnp.arange(NX)
    strip_index = row_index // SX
    offset = row_index % SX
    start_here = band_start[strip_index]
    in_band = (offset >= start_here) & (offset < start_here + 2 * ROWS_DEV)
    return jnp.where(in_band, SUB_MOST, background).astype(jnp.int32)


def touch_ends(result, key, smallest, largest):
    spot = [jax.random.randint(jax.random.fold_in(key, axis), (), 0, length) for axis, length in enumerate(result.shape)]
    main_axis = result.shape.index(max(result.shape))
    beside = spot[:main_axis] + [(spot[main_axis] + 1) % result.shape[main_axis]] + spot[main_axis + 1:]
    return result.at[tuple(spot)].set(smallest).at[tuple(beside)].set(largest)


def level_of(stream_key, shape, pieces, smallest, high):
    level = 1.0
    for dim, blocks in pieces:
        draws = jax.random.uniform(jax.random.fold_in(jax.random.fold_in(stream_key, 6), dim), (blocks,), jnp.float32, smallest / len(pieces), high / len(pieces))
        level = level * jnp.repeat(jnp.exp(draws), shape[dim] // blocks).reshape((-1,) + (1,) * (len(shape) - 1 - dim))
    return level


def noise(own_key, shape, scale, reach, cuts=(), kind=jnp.bfloat16):
    drawn = scale * jax.random.normal(own_key, shape, jnp.float32)
    if cuts:
        drawn = drawn * level_of(own_key, shape, cuts, -0.22, 0.18)
    return jnp.clip(drawn, -reach, reach).astype(kind)


def setup_inputs(seed: int = 0) -> dict:
    key_of = jax.random.split(jax.random.key(seed), 9)
    return {
        "spectrum": jnp.clip(jnp.exp(math.log(2.0) - 3.6888794 * jax.random.uniform(key_of[0], (NC, NX, NY), jnp.float32) ** level_of(key_of[0], (NC, NX, NY), ((0, 16), (1, 8)), -0.2, 0.2)), 0.05, 2.0),
        "mask": touch_ends((jax.random.randint(key_of[1], (NX, NY), 0, 10) < 7).astype(jnp.int32), jax.random.fold_in(key_of[1], 1), 0, 1),
        "depth_level": touch_ends(jax.random.randint(key_of[2], (NX, NY), 0, LEVELS), jax.random.fold_in(key_of[2], 1), 0, LEVELS - 1).astype(jnp.int32),
        "speed_table": jnp.clip(jnp.exp(jax.random.uniform(key_of[3], (NF, LEVELS), jnp.float32, math.log(0.2), math.log(1.8))), 0.2, 1.8),
        "wind_u": noise(key_of[4], (NX, NY), 1.0, 4.0, ((0, 8),), jnp.float32),
        "wind_v": noise(key_of[5], (NX, NY), 1.0, 4.0, ((0, 8),), jnp.float32),
        "substeps": draw_substeps(jax.random.fold_in(key_of[8], 71), 0),
        "coupling": noise(key_of[7], (NC, NC), NC ** -0.5, 0.15625),
    }


TIME_STEP = 1.0
WIND_RATE = 0.3
BREAK_RATE = 0.8
MIXING = 0.5


def spectral_tables(component_index):
    frequency = component_index // ND
    direction = component_index % ND
    direction_angle = (2.0 * math.pi / ND) * (direction.astype(jnp.float32) + 0.5)
    freq_value = frequency.astype(jnp.float32)
    phase_speed = 1.5 * jnp.power(1.1, -freq_value)
    norm_total = ND * jnp.sum(jnp.power(1.1, 2.0 * jnp.arange(NF).astype(jnp.float32)))
    weight = jnp.power(1.1, 2.0 * freq_value) / norm_total
    damping = BREAK_RATE * (freq_value + 1.0) / NF
    return jnp.cos(direction_angle), jnp.sin(direction_angle), phase_speed, weight, damping


def upwind_sweep(padded, courant, grid_dim):
    extent = courant.shape[grid_dim]

    def window_at(offset):
        return lax.slice_in_dim(padded, offset, offset + extent, axis=grid_dim)

    centre = window_at(2)
    forward = courant >= 0.0
    upwind_near = jnp.where(forward, window_at(1), window_at(3))
    upwind_far = jnp.where(forward, window_at(0), window_at(4))
    magnitude = jnp.abs(courant)
    return (centre - 0.5 * magnitude * (3.0 * centre - 4.0 * upwind_near + upwind_far)
            + 0.5 * magnitude * magnitude * (centre - 2.0 * upwind_near + upwind_far))


def source_row(wave_field, east_wind, north_wind, turns, coupling, tables):
    cos_part, sin_part, phase_speed, weight, damping = tables
    rate_in = WIND_RATE * jnp.maximum(0.0, east_wind[None, :] * cos_part[:, None]
                                      + north_wind[None, :] * sin_part[:, None] - phase_speed[:, None])
    step_size = TIME_STEP / turns.astype(jnp.float32)

    def advance(repeat, current):
        steepness = jnp.sum(weight[:, None] * current, axis=0)
        dissipation = damping[:, None] * (steepness * steepness)[None, :]
        interaction = jnp.dot(coupling, current.astype(jnp.bfloat16), preferred_element_type=jnp.float32)
        return current + step_size * ((rate_in - dissipation) * current + MIXING * interaction)

    return lax.fori_loop(0, turns, advance, wave_field)


def reference(spectrum, mask, depth_level, speed_table, wind_u, wind_v, substeps, coupling):
    sea_mask = mask.astype(jnp.float32)
    everyone = jnp.arange(NF * ND, dtype=jnp.int32)
    tables = spectral_tables(everyone)
    cos_part, sin_part = tables[0], tables[1]
    level_hot = (depth_level[None] == jnp.arange(LEVELS, dtype=jnp.int32)[:, None, None]).astype(jnp.float32)

    def propagate(frequency):
        freq_block = lax.dynamic_slice_in_dim(spectrum, frequency * ND, ND, 0) * sea_mask[None]
        table_row = lax.dynamic_index_in_dim(speed_table, frequency, 0, keepdims=False)
        base_speed = jnp.einsum('l,lxy->xy', table_row, level_hot, precision=lax.Precision.HIGHEST)
        padded = jnp.pad(freq_block, ((0, 0), (2, 2), (0, 0)))
        freq_block = upwind_sweep(padded, base_speed[None] * cos_part[:ND, None, None], 1) * sea_mask[None]
        padded = jnp.pad(freq_block, ((0, 0), (0, 0), (2, 2)))
        return upwind_sweep(padded, base_speed[None] * sin_part[:ND, None, None], 2) * sea_mask[None]

    propagated = lax.map(propagate, jnp.arange(NF, dtype=jnp.int32)).reshape(NF * ND, NX, NY)
    rows_first = jnp.transpose(propagated, (1, 0, 2))

    def per_row(row_items):
        wave_field, east_wind, north_wind, turns = row_items
        return source_row(wave_field, east_wind, north_wind, turns, coupling, tables)

    updated = lax.map(per_row, (rows_first, wind_u, wind_v, substeps))
    return jnp.transpose(updated, (1, 0, 2))
```

```python
import math

import jax
import jax.numpy as jnp
import numpy as np
from jax import lax
from jax.experimental import pallas as pl
from jax.experimental.pallas import tpu as pltpu
from jax.sharding import PartitionSpec as P

NF = 36
ND = 36
LEVELS = 8

TIME_STEP = 1.0
WIND_RATE = 0.3
BREAK_RATE = 0.8
MIXING = 0.5

LANES = 128
SUBS = 8
VMEM_LIMIT = 56 * 1024 * 1024


def edge_rows(cells, axis, width):
    count = lax.axis_size(axis)
    ends = count - 1
    head = cells[:, :width]
    tail = cells[:, -width:]
    below = lax.ppermute(tail, axis, [(i, i + 1) for i in range(ends)])
    above = lax.ppermute(head, axis, [(i + 1, i) for i in range(ends)])
    return below, above


def spectral_tables():
    frequency = np.arange(NF, dtype=np.float64)
    angle = 2.0 * math.pi / ND * (np.arange(ND) + 0.5)
    norm_total = ND * np.sum(np.power(1.1, 2.0 * frequency))
    by_frequency = np.stack([
        WIND_RATE * 1.5 * np.power(1.1, -frequency),
        np.power(1.1, 2.0 * frequency) / norm_total,
        BREAK_RATE * (frequency + 1.0) / NF,
    ])
    by_direction = np.zeros((4 * ND, SUBS))
    by_direction[:, 0] = WIND_RATE * np.tile(np.cos(angle), 4)
    by_direction[:, 1] = WIND_RATE * np.tile(np.sin(angle), 4)
    return jnp.asarray(by_frequency.astype(np.float32)), jnp.asarray(by_direction.astype(np.float32))


def take_lanes(values, index):
    return jnp.take_along_axis(values, index, axis=1, mode="promise_in_bounds")


class Layout:
    def __init__(self, rows, columns, hosts):
        self.tiles = rows // SUBS
        self.halves = columns // LANES
        self.hosts = hosts
        self.guests = [(t, h) for t in range(hosts, self.tiles) for h in range(self.halves)]
        self.blocks = [(t, h) for t in range(hosts) for h in range(self.halves)]
        self.guest_tiles = self.tiles - hosts
        self.share = hosts // self.guest_tiles if self.guest_tiles else hosts

    def guest_of(self, t, h):
        return (t // self.share) * self.halves + h

    def block_of(self, t, h):
        return t * self.halves + h


def view(ref, t, h):
    return ref[pl.ds(t * SUBS, SUBS), pl.ds(h * LANES, LANES)]


def make_plan(layout, mask, wind_u, wind_v, substeps):
    halves = layout.halves
    host_rows = layout.hosts * SUBS
    guest_rows = layout.guest_tiles * SUBS
    columns = halves * LANES

    def body(mask_ref, u_ref, v_ref, n_ref, fill_ref, spare_ref, back_ref, uo_ref, vo_ref, no_ref, spare_flag, back_flag):
        lane = lax.broadcasted_iota(jnp.int32, (SUBS, LANES), 1)

        def ranks(marked):
            total = marked
            for bit in range(7):
                step = 1 << bit
                total = total + jnp.where(lane >= step, pltpu.roll(total, step, 1), 0)
            rank = total - marked
            state = jnp.where(marked > 0, lane + LANES * (lane - rank), -1)
            for bit in range(7):
                moved = pltpu.roll(state, LANES - (1 << bit), 1)
                take = (moved >= 0) & (((moved >> (7 + bit)) & 1) == 1)
                stay = (state >= 0) & (((state >> (7 + bit)) & 1) == 0)
                state = jnp.where(take, moved, jnp.where(stay, state, -1))
            count = jnp.broadcast_to(jnp.sum(marked, axis=1, keepdims=True), (SUBS, LANES))
            return rank, jnp.maximum(state, 0) & (LANES - 1), count

        def inside(index):
            return jnp.clip(index, 0, LANES - 1)

        hole, hole_rank, hole_at, hole_count = [], [], [], []
        for t, h in layout.blocks:
            marked = 1 - view(mask_ref, t, h)
            rank, at, count = ranks(marked)
            hole.append(marked > 0)
            hole_rank.append(rank)
            hole_at.append(at)
            hole_count.append(count)
        sea, sea_rank, sea_at, sea_count = [], [], [], []
        for t, h in layout.guests:
            marked = view(mask_ref, t, h)
            rank, at, count = ranks(marked)
            sea.append(marked > 0)
            sea_rank.append(rank)
            sea_at.append(at)
            sea_count.append(count)

        guests = len(layout.guests)
        zero = jnp.zeros((SUBS, LANES), jnp.int32)
        start = []
        holes_of = [zero] * guests
        for b, (t, h) in enumerate(layout.blocks):
            j = layout.guest_of(t, h)
            start.append(holes_of[j])
            holes_of[j] = holes_of[j] + hole_count[b]
        open_of = [jnp.maximum(holes_of[j] - sea_count[j], 0) for j in range(guests)]
        left_of = [jnp.maximum(sea_count[j] - holes_of[j], 0) for j in range(guests)]
        open_start, left_start = [zero], [zero]
        for j in range(1, guests):
            open_start.append(open_start[-1] + open_of[j - 1])
            left_start.append(left_start[-1] + left_of[j - 1])

        for b, (t, h) in enumerate(layout.blocks):
            own = layout.guest_of(t, h)
            rank = start[b] + hole_rank[b]
            first = take_lanes(sea_at[own], inside(rank))
            spare = jnp.full((SUBS, LANES), -1, jnp.int32)
            extra = open_start[own] + rank - sea_count[own]
            loose = hole[b] & (rank >= sea_count[own])
            for j in range(guests):
                if j != own:
                    fits = loose & (extra >= left_start[j]) & (extra < left_start[j] + left_of[j])
                    found = take_lanes(sea_at[j], inside(extra - left_start[j] + holes_of[j]))
                    spare = jnp.where(fits, LANES * j + found, spare)
            place = (pl.ds(t * SUBS, SUBS), pl.ds(h * LANES, LANES))
            fill_ref[place] = first
            spare_ref[place] = spare
            spare_flag[b] = jnp.max(spare)
            filled = (rank < sea_count[own]) | (spare >= 0)
            for source, target in ((u_ref, uo_ref), (v_ref, vo_ref), (n_ref, no_ref)):
                value = take_lanes(view(source, *layout.guests[own]), first)
                for j, guest in enumerate(layout.guests):
                    if j != own:
                        other = take_lanes(view(source, *guest), spare & (LANES - 1))
                        value = jnp.where(spare >> 7 == j, other, value)
                if source is n_ref:
                    value = jnp.where(filled, value, 1.0)
                target[place] = jnp.where(hole[b], value, view(source, t, h))

        for j, (t, h) in enumerate(layout.guests):
            rank = sea_rank[j]
            back = jnp.full((SUBS, LANES), -1, jnp.int32)
            home = jnp.full((SUBS, LANES), 1, jnp.int32)
            extra = left_start[j] + rank - holes_of[j]
            for b, block in enumerate(layout.blocks):
                own = layout.guest_of(*block)
                if own == j:
                    at = rank
                    ok = sea[j] & (rank < holes_of[j])
                else:
                    at = extra - open_start[own] + sea_count[own]
                    ok = sea[j] & (rank >= holes_of[j])
                    ok = ok & (extra >= open_start[own]) & (extra < open_start[own] + open_of[own])
                ok = ok & (at >= start[b]) & (at < start[b] + hole_count[b])
                back = jnp.where(ok, LANES * b + take_lanes(hole_at[b], inside(at - start[b])), back)
                if own != j:
                    home = jnp.where(ok, 0, home)
            back_ref[pl.ds((t - layout.hosts) * SUBS, SUBS), pl.ds(h * LANES, LANES)] = back
            back_flag[j] = 1 - jnp.min(home)

    vmem = pl.BlockSpec(memory_space=pltpu.VMEM)
    smem = pl.BlockSpec(memory_space=pltpu.SMEM)
    whole = (host_rows, columns)
    turns = jnp.broadcast_to(substeps.astype(jnp.float32)[:, None], mask.shape)
    return pl.pallas_call(
        body,
        in_specs=[vmem] * 4,
        out_specs=[vmem] * 6 + [smem] * 2,
        out_shape=[
            jax.ShapeDtypeStruct(whole, jnp.int32),
            jax.ShapeDtypeStruct(whole, jnp.int32),
            jax.ShapeDtypeStruct((guest_rows, columns), jnp.int32),
            jax.ShapeDtypeStruct(whole, jnp.float32),
            jax.ShapeDtypeStruct(whole, jnp.float32),
            jax.ShapeDtypeStruct(whole, jnp.float32),
            jax.ShapeDtypeStruct((len(layout.blocks),), jnp.int32),
            jax.ShapeDtypeStruct((len(layout.guests),), jnp.int32),
        ],
        name="plan",
    )(mask, wind_u, wind_v, turns)


def wire_rows(layout, per_group):
    even = per_group // SUBS * SUBS
    rest = per_group - even
    return layout.hosts * even, -(-(layout.hosts * per_group) // SUBS) * SUBS, even, rest


def propagate(layout, spectrum, below, above, mask, depth_level, speed_table, group_index, plan):
    per_group, rows, columns = spectrum.shape
    groups = SUBS * layout.halves
    rest_start, pitch, even, rest = wire_rows(layout, per_group)
    steps = even // SUBS + 1
    kinds = (per_group - 2) // ND + 2
    angle = 2.0 * math.pi / ND * (np.arange(ND) + 0.5)
    turns = jnp.asarray(np.stack([np.cos(angle), np.sin(angle)]).astype(np.float32))
    packed = layout.guest_tiles > 0

    def body(*refs):
        if packed:
            (first_ref, turn_ref, speed_ref, flag_ref, spec_ref, below_ref, above_ref, mask_ref, depth_ref,
             fill_ref, spare_ref, out_ref, base_ref, sea_ref, pad_ref, field_ref) = refs
        else:
            (first_ref, turn_ref, speed_ref, spec_ref, below_ref, above_ref, mask_ref, depth_ref,
             out_ref, base_ref, sea_ref, pad_ref, field_ref) = refs
        step = pl.program_id(0)
        first = first_ref[0]
        lowest = first // ND

        @pl.when(step == 0)
        def _():
            sea_ref[...] = mask_ref[...].astype(jnp.float32)
            for k in range(kinds):
                f = jnp.minimum(lowest + k, NF - 1)
                for t in range(layout.tiles):
                    place = pl.ds(t * SUBS, SUBS)
                    level = depth_ref[place, :]
                    speed = jnp.zeros(level.shape, jnp.float32)
                    for l in range(LEVELS):
                        speed = jnp.where(level == l, speed_ref[f, l], speed)
                    base_ref[k, place, :] = speed

        lane = lax.broadcasted_iota(jnp.int32, (2 * SUBS, columns), 1)

        def sweep(centre, near, far, amount):
            one = amount * (2.0 - amount)
            two = 0.5 * amount * (amount - 1.0)
            return centre + one * (near - centre) + two * (far - centre)

        def component(cc, carry):
            c = first + step * SUBS + cc
            d = c % ND
            kind = c // ND - lowest
            cos_part = turn_ref[0, d]
            sin_part = turn_ref[1, d]
            wide_x = jnp.abs(cos_part)
            wide_y = jnp.abs(sin_part)
            pad_ref[pl.ds(SUBS - 2, 2), :] = below_ref[cc]
            pad_ref[pl.ds(rows + SUBS, 2), :] = above_ref[cc]
            pad_ref[pl.ds(SUBS, rows), :] = spec_ref[cc] * sea_ref[...]

            def run(sign_x, sign_y):
                for t in range(0, layout.tiles, 2):
                    place = pl.ds(t * SUBS, 2 * SUBS)
                    base = base_ref[kind, place, :]
                    at = (t + 1) * SUBS
                    centre = pad_ref[pl.ds(at, 2 * SUBS), :]
                    near = pad_ref[pl.ds(at - sign_x, 2 * SUBS), :]
                    far = pad_ref[pl.ds(at - 2 * sign_x, 2 * SUBS), :]
                    centre = sweep(centre, near, far, base * wide_x) * sea_ref[place, :]
                    near = pltpu.roll(centre, sign_y % columns, 1)
                    far = pltpu.roll(centre, (2 * sign_y) % columns, 1)
                    if sign_y > 0:
                        near = jnp.where(lane >= 1, near, 0.0)
                        far = jnp.where(lane >= 2, far, 0.0)
                    else:
                        near = jnp.where(lane < columns - 1, near, 0.0)
                        far = jnp.where(lane < columns - 2, far, 0.0)
                    field_ref[cc, place, :] = sweep(centre, near, far, base * wide_y)

            for sign_x in (1, -1):
                for sign_y in (1, -1):
                    right_x = cos_part >= 0.0 if sign_x > 0 else cos_part < 0.0
                    right_y = sin_part >= 0.0 if sign_y > 0 else sin_part < 0.0

                    @pl.when(right_x & right_y)
                    def _():
                        run(sign_x, sign_y)

            return carry

        lax.fori_loop(0, jnp.where(step == steps - 1, rest, SUBS), component, 0)

        def pack(count, row_of):
            for b, (t, h) in enumerate(layout.blocks):
                place = (pl.ds(t * SUBS, SUBS), pl.ds(h * LANES, LANES))

                def put(cc, value):
                    out_ref[pl.ds(h * SUBS * pitch + row_of(t, cc), SUBS, stride=pitch), :] = value

                if not packed:
                    for cc in range(count):
                        put(cc, field_ref[(cc,) + place])
                    continue
                own = layout.guests[layout.guest_of(t, h)]
                sea = sea_ref[place] > 0.0
                first = fill_ref[place]

                def base_value(cc):
                    guest = view(field_ref.at[cc], *own)
                    return jnp.where(sea, field_ref[(cc,) + place], take_lanes(guest, first))

                @pl.when(flag_ref[b] < 0)
                def _():
                    for cc in range(count):
                        put(cc, base_value(cc))

                @pl.when(flag_ref[b] >= 0)
                def _():
                    spare = spare_ref[place]
                    for cc in range(count):
                        value = base_value(cc)
                        for j, guest in enumerate(layout.guests):
                            other = take_lanes(view(field_ref.at[cc], *guest), spare & (LANES - 1))
                            value = jnp.where(spare >> 7 == j, other, value)
                        put(cc, value)

        @pl.when(step < steps - 1)
        def _():
            pack(SUBS, lambda t, cc: t * even + step * SUBS + cc)

        @pl.when(step == steps - 1)
        def _():
            pack(rest, lambda t, cc: rest_start + t * rest + cc)

    smem = pl.BlockSpec(memory_space=pltpu.SMEM)

    def fixed(array):
        return pl.BlockSpec(array.shape, lambda i: (0,) * array.ndim)

    extra_smem = [plan["spare_flag"]] if packed else []
    extra = [plan["fill"], plan["spare"]] if packed else []
    chunked = pl.BlockSpec((SUBS, rows, columns), lambda i: (i, 0, 0))
    edge = pl.BlockSpec((SUBS, 2, columns), lambda i: (i, 0, 0))
    wire = pl.pallas_call(
        body,
        grid=(steps,),
        in_specs=[smem] * (3 + len(extra_smem)) + [chunked, edge, edge, fixed(mask), fixed(depth_level)] + [fixed(a) for a in extra],
        out_specs=pl.BlockSpec((groups * pitch, LANES), lambda i: (0, 0)),
        out_shape=jax.ShapeDtypeStruct((groups * pitch, LANES), jnp.float32),
        scratch_shapes=[
            pltpu.VMEM((kinds, rows, columns), jnp.float32),
            pltpu.VMEM((rows, columns), jnp.float32),
            pltpu.VMEM((rows + 2 * SUBS, columns), jnp.float32),
            pltpu.VMEM((SUBS, rows, columns), jnp.float32),
        ],
        compiler_params=pltpu.CompilerParams(vmem_limit_bytes=VMEM_LIMIT, dimension_semantics=("arbitrary",)),
        name="propagate",
    )((group_index * per_group).reshape(1), turns, speed_table, *extra_smem, spectrum, below, above, mask, depth_level, *extra)
    return wire.reshape(groups, pitch, LANES)


def apply_source(layout, wire, per_group, east, north, turns, coupling):
    groups, pitch, _ = wire.shape
    rest_start, _, even, rest = wire_rows(layout, per_group)
    total = groups * per_group
    pairs = layout.hosts // 2
    wide = 2 * LANES
    span = 4 * ND
    most = jnp.max(turns.reshape(pairs, wide), axis=1).astype(jnp.int32)
    by_frequency, by_direction = spectral_tables()

    def body(most_ref, freq_ref, wire_ref, east_ref, north_ref, turn_ref, coupling_ref, dir_ref, out_ref,
             value_ref, round_ref, wind_ref, mix_ref):
        subrow = lax.broadcasted_iota(jnp.int32, (SUBS, wide), 0)

        def moves():
            for k in range(groups):
                yield (k * per_group, even), lambda t, k=k: (k * pitch + t * even, even)
                yield (k * per_group + even, rest), lambda t, k=k: (k * pitch + rest_start + t * rest, rest)

        def per_row(row, start, stop):
            def at(kind):
                low, high = start // ND, (stop - 1) // ND
                first = freq_ref[kind, row + low]
                if low == high:
                    return first
                return jnp.where(subrow < high * ND - start, first, freq_ref[kind, row + high])
            return at

        for pair in range(pairs):
            for half in range(2):
                lanes = pl.ds(half * LANES, LANES)
                for here, there in moves():
                    value_ref[pl.ds(*here), lanes] = wire_ref[pl.ds(*there(2 * pair + half)), :]

            def line(ref):
                row = jnp.concatenate([ref[pl.ds(2 * pair, 1), :], ref[pl.ds(2 * pair + 1, 1), :]], axis=1)
                return jnp.broadcast_to(row, (SUBS, wide))

            east_line, north_line, turn_line = line(east_ref), line(north_ref), line(turn_ref)
            step_line = TIME_STEP / turn_line
            for i in range(0, span, SUBS):
                columns = dir_ref[pl.ds(i, SUBS), :]
                wind_ref[pl.ds(i, SUBS), :] = east_line * columns[:, 0:1] + north_line * columns[:, 1:2]

            def sweep(change):
                def block(i, steep):
                    for q in range(0, span, 2 * SUBS):
                        values = []
                        for start in (q, q + SUBS):
                            at = per_row(i * 4, start, start + SUBS)
                            place = pl.ds(pl.multiple_of(i * span + start, SUBS), SUBS)
                            value = value_ref[place, :]
                            if change is not None:
                                value = change(place, start, at, value)
                                value_ref[place, :] = value
                            steep = steep + at(1) * value
                            values.append(value)
                        both = pl.ds(pl.multiple_of(i * span + q, 2 * SUBS), 2 * SUBS)
                        round_ref[both, :] = jnp.concatenate(values, axis=0).astype(jnp.bfloat16)
                    return steep

                steep = lax.fori_loop(0, total // span, block, jnp.zeros((SUBS, wide), jnp.float32))
                steepness = jnp.broadcast_to(jnp.sum(steep, axis=0, keepdims=True), (SUBS, wide))
                return steepness * steepness

            def turn(repeat, square):
                mix_ref[...] = jnp.dot(coupling_ref[...], round_ref[...], preferred_element_type=jnp.float32)
                active = repeat.astype(jnp.float32) < turn_line
                half_step = MIXING * step_line

                def change(place, start, at, value):
                    rate = jnp.maximum(0.0, wind_ref[pl.ds(start, SUBS), :] - at(0)) - at(2) * square
                    return jnp.where(active, value + (step_line * (rate * value) + half_step * mix_ref[place, :]), value)

                return sweep(change)

            lax.fori_loop(0, most_ref[pair], turn, sweep(None))
            for half in range(2):
                lanes = pl.ds(half * LANES, LANES)
                for here, there in moves():
                    out_ref[pl.ds(*there(2 * pair + half)), :] = value_ref[pl.ds(*here), lanes]

    vmem = pl.BlockSpec(memory_space=pltpu.VMEM)
    smem = pl.BlockSpec(memory_space=pltpu.SMEM)
    out = pl.pallas_call(
        body,
        in_specs=[smem] * 2 + [vmem] * 6,
        out_specs=vmem,
        out_shape=jax.ShapeDtypeStruct((groups * pitch, LANES), jnp.float32),
        scratch_shapes=[
            pltpu.VMEM((total, wide), jnp.float32),
            pltpu.VMEM((total, wide), jnp.bfloat16),
            pltpu.VMEM((span, wide), jnp.float32),
            pltpu.VMEM((total, wide), jnp.float32),
        ],
        compiler_params=pltpu.CompilerParams(vmem_limit_bytes=VMEM_LIMIT),
        name="source",
    )(most, by_frequency, wire.reshape(groups * pitch, LANES), east, north, turns, coupling, by_direction)
    return out.reshape(groups, pitch, LANES)


def unpack(layout, wire, per_group, mask, plan):
    groups, pitch, _ = wire.shape
    rest_start, _, even, rest = wire_rows(layout, per_group)
    steps = even // SUBS + 1
    rows, columns = mask.shape
    packed = layout.guest_tiles > 0

    def body(*refs):
        if packed:
            flag_ref, wire_ref, mask_ref, back_ref, out_ref = refs
        else:
            wire_ref, mask_ref, out_ref = refs
        step = pl.program_id(0)

        def spread(count, row_of):
            def get(t, h, cc):
                return wire_ref[pl.ds(h * SUBS * pitch + row_of(t, cc), SUBS, stride=pitch), :]

            for t, h in layout.blocks:
                place = (pl.ds(t * SUBS, SUBS), pl.ds(h * LANES, LANES))
                sea = mask_ref[place] > 0
                for cc in range(count):
                    out_ref[(cc,) + place] = jnp.where(sea, get(t, h, cc), 0.0)
            for j, (t, h) in enumerate(layout.guests):
                place = (pl.ds(t * SUBS, SUBS), pl.ds(h * LANES, LANES))
                back = back_ref[pl.ds((t - layout.hosts) * SUBS, SUBS), pl.ds(h * LANES, LANES)]
                index = back & (LANES - 1)
                block = back >> 7

                def fetch(blocks):
                    for cc in range(count):
                        value = jnp.zeros((SUBS, LANES), jnp.float32)
                        for b in blocks:
                            found = take_lanes(get(*layout.blocks[b], cc), index)
                            value = jnp.where(block == b, found, value)
                        out_ref[(cc,) + place] = value

                near = [b for b, at in enumerate(layout.blocks) if layout.guest_of(*at) == j]

                @pl.when(flag_ref[j] == 0)
                def _():
                    fetch(near)

                @pl.when(flag_ref[j] != 0)
                def _():
                    fetch(range(len(layout.blocks)))

        @pl.when(step < steps - 1)
        def _():
            spread(SUBS, lambda t, cc: t * even + step * SUBS + cc)

        @pl.when(step == steps - 1)
        def _():
            spread(rest, lambda t, cc: rest_start + t * rest + cc)

    smem = pl.BlockSpec(memory_space=pltpu.SMEM)
    fixed = pl.BlockSpec((groups * pitch, LANES), lambda i: (0, 0))
    fixed_mask = pl.BlockSpec((rows, columns), lambda i: (0, 0))
    extra_smem = [plan["back_flag"]] if packed else []
    extra = [plan["back"]] if packed else []
    return pl.pallas_call(
        body,
        grid=(steps,),
        in_specs=[smem] * len(extra_smem) + [fixed, fixed_mask] + [pl.BlockSpec(a.shape, lambda i: (0, 0)) for a in extra],
        out_specs=pl.BlockSpec((SUBS, rows, columns), lambda i: (i, 0, 0)),
        out_shape=jax.ShapeDtypeStruct((per_group, rows, columns), jnp.float32),
        compiler_params=pltpu.CompilerParams(vmem_limit_bytes=VMEM_LIMIT, dimension_semantics=("arbitrary",)),
        name="unpack",
    )(*extra_smem, wire.reshape(groups * pitch, LANES), mask, *extra)


def regroup(wire):
    return lax.all_to_all(wire, "comp", split_axis=0, concat_axis=0, tiled=True)


def on_device(spectrum, mask, depth_level, speed_table, wind_u, wind_v, substeps, coupling):
    per_group, rows, columns = spectrum.shape
    group_index = lax.axis_index("comp")
    tiles = rows // SUBS
    edges = jnp.concatenate([spectrum[:, :2], spectrum[:, -2:]], axis=1) * jnp.concatenate([mask[:2], mask[-2:]], axis=0).astype(jnp.float32)[None]
    below, above = edge_rows(edges, "space", 2)
    subrow = group_index % SUBS
    half = group_index // SUBS

    def own(array, hosts):
        parts = array.reshape(hosts, SUBS, columns // LANES, LANES)
        return lax.dynamic_slice(parts, (0, subrow, half, 0), (hosts, 1, 1, LANES)).reshape(hosts, LANES)

    def step(hosts):
        layout = Layout(rows, columns, hosts)
        if hosts < tiles:
            fill, spare, back, east, north, turns, spare_flag, back_flag = make_plan(layout, mask, wind_u, wind_v, substeps)
            plan = dict(fill=fill, spare=spare, back=back, spare_flag=spare_flag, back_flag=back_flag)
        else:
            plan = {}
            east, north = wind_u, wind_v
            turns = jnp.broadcast_to(substeps.astype(jnp.float32)[:, None], mask.shape)
        wire = propagate(layout, spectrum, below, above, mask, depth_level, speed_table, group_index, plan)
        wire = regroup(wire)
        wire = apply_source(layout, wire, per_group, own(east, hosts), own(north, hosts), own(turns, hosts), coupling)
        wire = regroup(wire)
        return unpack(layout, wire, per_group, mask, plan)

    hosts = tiles * 3 // 4
    busy = jnp.sum(mask.reshape(tiles, SUBS, columns), axis=(0, 2))
    return lax.cond(jnp.all(busy <= hosts * columns), lambda: step(hosts), lambda: step(tiles))


def solution(mesh):
    placed = (
        P("comp", "space", None),
        P("space", None),
        P("space", None),
        P(),
        P("space", None),
        P("space", None),
        P("space"),
        P(),
    )
    return jax.shard_map(
        on_device, mesh=mesh, in_specs=placed, out_specs=P("comp", "space", None), check_vma=False
    )
```

```python
import math

import jax
import jax.numpy as jnp
import numpy as np
from jax import lax
from jax.experimental import pallas as pl
from jax.experimental.pallas import tpu as pltpu
from jax.sharding import PartitionSpec as P

NF = 36
ND = 36
LEVELS = 8

TIME_STEP = 1.0
WIND_RATE = 0.3
BREAK_RATE = 0.8
MIXING = 0.5

LANES = 128
SUBS = 8
VMEM_LIMIT = 56 * 1024 * 1024


def edge_rows(cells, axis, width):
    count = lax.axis_size(axis)
    ends = count - 1
    head = cells[:, :width]
    tail = cells[:, -width:]
    below = lax.ppermute(tail, axis, [(i, i + 1) for i in range(ends)])
    above = lax.ppermute(head, axis, [(i + 1, i) for i in range(ends)])
    return below, above


def spectral_tables(period):
    frequency = np.arange(NF, dtype=np.float64)
    angle = 2.0 * math.pi / ND * (np.arange(ND) + 0.5)
    norm_total = ND * np.sum(np.power(1.1, 2.0 * frequency))
    phase = WIND_RATE * 1.5 * np.power(1.1, -frequency)
    weight = np.power(1.1, 2.0 * frequency) / norm_total
    damping = BREAK_RATE * (frequency + 1.0) / NF
    by_direction = np.zeros((period, SUBS))
    by_direction[:, 0] = WIND_RATE * np.tile(np.cos(angle), period // ND)
    by_direction[:, 1] = WIND_RATE * np.tile(np.sin(angle), period // ND)
    return phase, weight, damping, jnp.asarray(by_direction.astype(np.float32))


def take_lanes(values, index):
    return jnp.take_along_axis(values, index, axis=1, mode="promise_in_bounds")


class Layout:
    def __init__(self, rows, columns, hosts, guests):
        self.tiles = rows // SUBS
        self.halves = columns // LANES
        self.hosts = hosts
        self.guest_tiles = guests
        self.guests = [(t, h) for t in guests for h in range(self.halves)]
        self.blocks = [(i, h) for i in range(len(hosts)) for h in range(self.halves)]
        self.share = len(hosts) // len(guests) if guests else 0

    def guest_of(self, i, h):
        return (i // self.share) * self.halves + h


def view(ref, t, h):
    return ref[pl.ds(t * SUBS, SUBS), pl.ds(h * LANES, LANES)]


def count_blocks(layout, mask_ref):
    marked = [1 - view(mask_ref, layout.hosts[i], h) for i, h in layout.blocks]
    marked = jnp.concatenate(marked + [view(mask_ref, t, h) for t, h in layout.guests], axis=0)
    lane = lax.broadcasted_iota(jnp.int32, marked.shape, 1)
    upto = (lax.broadcasted_iota(jnp.int32, (LANES, LANES), 0) <= lax.broadcasted_iota(jnp.int32, (LANES, LANES), 1)).astype(jnp.bfloat16)
    total = jnp.dot(marked.astype(jnp.bfloat16), upto, preferred_element_type=jnp.float32).astype(jnp.int32)
    rank = total - marked
    state = jnp.where(marked > 0, lane + LANES * (lane - rank), -1)
    for bit in range(7):
        moved = pltpu.roll(state, LANES - (1 << bit), 1)
        take = (moved >= 0) & (((moved >> (7 + bit)) & 1) == 1)
        stay = (state >= 0) & (((state >> (7 + bit)) & 1) == 0)
        state = jnp.where(take, moved, jnp.where(stay, state, -1))
    place = jnp.maximum(state, 0) & (LANES - 1)
    count = jnp.broadcast_to(total[:, LANES - 1:], marked.shape)

    def parts(array):
        each = [array[i:i + SUBS] for i in range(0, array.shape[0], SUBS)]
        return each[:len(layout.blocks)], each[len(layout.blocks):]

    return parts(marked), parts(rank), parts(place), parts(count)


class Plan:
    def __init__(self, layout, mask_ref):
        (hole, self.sea), (self.hole_rank, self.sea_rank), (self.hole_at, self.sea_at), counts = count_blocks(layout, mask_ref)
        self.hole_count, self.sea_count = counts
        self.hole = [m > 0 for m in hole]
        self.sea = [m > 0 for m in self.sea]
        guests = len(layout.guests)
        zero = jnp.zeros((SUBS, LANES), jnp.int32)
        self.start = []
        self.holes_of = [zero] * guests
        for b, at in enumerate(layout.blocks):
            j = layout.guest_of(*at)
            self.start.append(self.holes_of[j])
            self.holes_of[j] = self.holes_of[j] + self.hole_count[b]
        self.open_of = [jnp.maximum(self.holes_of[j] - self.sea_count[j], 0) for j in range(guests)]
        self.left_of = [jnp.maximum(self.sea_count[j] - self.holes_of[j], 0) for j in range(guests)]
        self.open_start, self.left_start = [zero], [zero]
        for j in range(1, guests):
            self.open_start.append(self.open_start[-1] + self.open_of[j - 1])
            self.left_start.append(self.left_start[-1] + self.left_of[j - 1])


def inside(index):
    return jnp.clip(index, 0, LANES - 1)


VMEM_SPEC = pl.BlockSpec(memory_space=pltpu.VMEM)
SMEM_SPEC = pl.BlockSpec(memory_space=pltpu.SMEM)


def make_plan(layout, mask, wind_u, wind_v, substeps):
    columns = mask.shape[1]

    def body(mask_ref, u_ref, v_ref, n_ref, fill_ref, spare_ref, back_ref, uo_ref, vo_ref, no_ref, flag_ref, back_flag, fits_ref):
        p = Plan(layout, mask_ref)
        subrow = lax.broadcasted_iota(jnp.int32, (SUBS, LANES), 0)
        ranks = []

        def turns_of(t):
            result = jnp.zeros((SUBS, LANES), jnp.int32)
            for r in range(SUBS):
                result = jnp.where(subrow == r, n_ref[t * SUBS + r], result)
            return result.astype(jnp.float32)

        every = {t: turns_of(t) for t in range(layout.tiles)}
        for b, (i, h) in enumerate(layout.blocks):
            own = layout.guest_of(i, h)
            rank = p.start[b] + p.hole_rank[b]
            ranks.append(rank)
            first = take_lanes(p.sea_at[own], inside(rank))
            place = (pl.ds(i * SUBS, SUBS), pl.ds(h * LANES, LANES))
            fill_ref[place] = first
            flag_ref[b] = -1
            hole = p.hole[b]
            for source, target in ((u_ref, uo_ref), (v_ref, vo_ref)):
                value = take_lanes(view(source, *layout.guests[own]), first)
                target[place] = jnp.where(hole, value, view(source, layout.hosts[i], h))
            guest = jnp.where(rank < p.sea_count[own], every[layout.guests[own][0]], 1.0)
            no_ref[place] = jnp.where(hole, guest, every[layout.hosts[i]])

        for j, (t, h) in enumerate(layout.guests):
            rank = p.sea_rank[j]
            back = jnp.full((SUBS, LANES), -1, jnp.int32)
            for b, block in enumerate(layout.blocks):
                if layout.guest_of(*block) == j:
                    ok = p.sea[j] & (rank >= p.start[b]) & (rank < p.start[b] + p.hole_count[b])
                    back = jnp.where(ok, LANES * b + take_lanes(p.hole_at[b], inside(rank - p.start[b])), back)
            back_ref[pl.ds(layout.guest_tiles.index(t) * SUBS, SUBS), pl.ds(h * LANES, LANES)] = back
            back_flag[j] = 0

        left = sum(p.left_of)
        flag_ref[len(layout.blocks)] = jnp.max(left)
        fits_ref[0] = (jnp.max(left - sum(p.open_of)) <= 0).astype(jnp.int32)

        @pl.when(jnp.max(left) > 0)
        def _():
            for b, (i, h) in enumerate(layout.blocks):
                own = layout.guest_of(i, h)
                spare = jnp.full((SUBS, LANES), -1, jnp.int32)
                extra = p.open_start[own] + ranks[b] - p.sea_count[own]
                loose = p.hole[b] & (ranks[b] >= p.sea_count[own])
                for j in range(len(layout.guests)):
                    if j != own:
                        ok = loose & (extra >= p.left_start[j]) & (extra < p.left_start[j] + p.left_of[j])
                        found = take_lanes(p.sea_at[j], inside(extra - p.left_start[j] + p.holes_of[j]))
                        spare = jnp.where(ok, LANES * j + found, spare)
                place = (pl.ds(i * SUBS, SUBS), pl.ds(h * LANES, LANES))
                spare_ref[place] = spare
                most = jnp.max(spare)
                flag_ref[b] = most

                @pl.when(most >= 0)
                def _():
                    for j, guest in enumerate(layout.guests):
                        chosen = spare >> 7 == j
                        for source, target in ((u_ref, uo_ref), (v_ref, vo_ref)):
                            other = take_lanes(view(source, *guest), spare & (LANES - 1))
                            target[place] = jnp.where(chosen, other, target[place])
                        no_ref[place] = jnp.where(chosen, every[guest[0]], no_ref[place])

            for j, (t, h) in enumerate(layout.guests):
                @pl.when(jnp.max(p.left_of[j]) > 0)
                def _():
                    place = (pl.ds(layout.guest_tiles.index(t) * SUBS, SUBS), pl.ds(h * LANES, LANES))
                    back = back_ref[place]
                    rank = p.sea_rank[j]
                    extra = p.left_start[j] + rank - p.holes_of[j]
                    for b, block in enumerate(layout.blocks):
                        own = layout.guest_of(*block)
                        if own != j:
                            at = extra - p.open_start[own] + p.sea_count[own]
                            ok = p.sea[j] & (rank >= p.holes_of[j])
                            ok = ok & (extra >= p.open_start[own]) & (extra < p.open_start[own] + p.open_of[own])
                            ok = ok & (at >= p.start[b]) & (at < p.start[b] + p.hole_count[b])
                            back = jnp.where(ok, LANES * b + take_lanes(p.hole_at[b], inside(at - p.start[b])), back)
                    back_ref[place] = back
                    back_flag[j] = 1

    whole = (len(layout.hosts) * SUBS, columns)
    return pl.pallas_call(
        body,
        in_specs=[VMEM_SPEC] * 3 + [SMEM_SPEC],
        out_specs=[VMEM_SPEC] * 6 + [SMEM_SPEC] * 3,
        out_shape=[
            jax.ShapeDtypeStruct(whole, jnp.int32),
            jax.ShapeDtypeStruct(whole, jnp.int32),
            jax.ShapeDtypeStruct((len(layout.guest_tiles) * SUBS, columns), jnp.int32),
            jax.ShapeDtypeStruct(whole, jnp.float32),
            jax.ShapeDtypeStruct(whole, jnp.float32),
            jax.ShapeDtypeStruct(whole, jnp.float32),
            jax.ShapeDtypeStruct((len(layout.blocks) + 1,), jnp.int32),
            jax.ShapeDtypeStruct((len(layout.guests),), jnp.int32),
            jax.ShapeDtypeStruct((1,), jnp.int32),
        ],
        name="plan",
    )(mask, wind_u, wind_v, substeps)


class Wire:
    def __init__(self, layout, per_group, tiles):
        self.tiles = tiles
        self.even = per_group // SUBS * SUBS
        self.rest = per_group - self.even
        self.rest_start = len(tiles) * self.even
        self.pitch = -(-(len(tiles) * per_group) // SUBS) * SUBS
        self.groups = SUBS * layout.halves
        self.blocks = [b for b, (i, h) in enumerate(layout.blocks) if i in tiles]

    def row(self, t, c):
        t = t - self.tiles[0]
        return jnp.where(c < self.even, t * self.even + c, self.rest_start + t * self.rest + c - self.even)

    def lines(self, t, h, c):
        return pl.ds(h * SUBS * self.pitch + self.row(t, c), SUBS, stride=self.pitch)


def propagate(layout, wire, spectrum, edges, mask, depth_level, speed_table, group_index, filling):
    per_group, rows, columns = spectrum.shape
    run = ND // 4
    steps = per_group // run
    angle = 2.0 * math.pi / ND * (np.arange(ND) + 0.5)
    turns = jnp.asarray(np.abs(np.stack([np.cos(angle), np.sin(angle)])).astype(np.float32))
    packed = len(layout.guests) > 0
    tiles = sorted([layout.hosts[i] for i in wire.tiles] + layout.guest_tiles)
    edged = len(edges) > 0

    def body(*refs):
        refs = list(refs)
        first_ref, turn_ref, speed_ref = refs[:3]
        flag_ref = refs[3] if packed else None
        refs = refs[3 + packed:]
        spec_ref = refs[0]
        below_ref, above_ref = refs[1:3] if edged else (None, None)
        refs = refs[1 + 2 * edged:]
        mask_ref, depth_ref = refs[:2]
        fill_ref, spare_ref = refs[2:4] if packed else (None, None)
        out_ref, base_ref, sea_ref, pad_ref, field_ref = refs[2 + 2 * packed:]
        step = pl.program_id(0)
        start = first_ref[0] + step * run
        f = start // ND

        @pl.when(step == 0)
        def _():
            sea_ref[...] = mask_ref[...].astype(jnp.float32)

        @pl.when((step == 0) | (start % ND == 0))
        def _():
            for t in tiles:
                place = pl.ds(t * SUBS, SUBS)
                level = depth_ref[place, :]
                speed = jnp.zeros(level.shape, jnp.float32)
                for l in range(LEVELS):
                    speed = jnp.where(level == l, speed_ref[l, f], speed)
                base_ref[place, :] = speed

        lane = lax.broadcasted_iota(jnp.int32, (SUBS, LANES), 1)

        def sweep(centre, near, far, amount):
            one = amount * (2.0 - amount)
            two = 0.5 * amount * (amount - 1.0)
            return centre + one * (near - centre) + two * (far - centre)

        def shifted(parts, by):
            turned = [pltpu.roll(part, by % LANES, 1) for part in parts]
            edge = jnp.zeros_like(turned[0])
            if by > 0:
                return [jnp.where(lane >= by, turned[i], turned[i - 1] if i else edge) for i in range(len(parts))]
            ends = turned[1:] + [edge]
            return [jnp.where(lane < LANES + by, turned[i], ends[i]) for i in range(len(parts))]

        def run_all(sign_x, sign_y):
            def component(cc, carry):
                d = start % ND + cc
                wide_x = turn_ref[0, d]
                wide_y = turn_ref[1, d]
                needed = sorted({n for t in tiles for n in (t, t - sign_x) if 0 <= n < layout.tiles})
                if edged:
                    pad_ref[cc, pl.ds(SUBS - 2, 2), :] = below_ref[step * run + cc]
                    pad_ref[cc, pl.ds(rows + SUBS, 2), :] = above_ref[step * run + cc]
                for t in needed:
                    place = pl.ds(t * SUBS, SUBS)
                    pad_ref[cc, pl.ds((t + 1) * SUBS, SUBS), :] = spec_ref[cc, place, :] * sea_ref[place, :]
                for t in tiles:
                    place = pl.ds(t * SUBS, SUBS)
                    at = (t + 1) * SUBS
                    base = base_ref[place, :]
                    centre = pad_ref[cc, pl.ds(at, SUBS), :]
                    near = pad_ref[cc, pl.ds(at - sign_x, SUBS), :]
                    far = pad_ref[cc, pl.ds(at - 2 * sign_x, SUBS), :]
                    centre = sweep(centre, near, far, base * wide_x) * sea_ref[place, :]
                    amount = base * wide_y
                    parts = [centre[:, h * LANES:(h + 1) * LANES] for h in range(layout.halves)]
                    near = shifted(parts, sign_y)
                    far = shifted(parts, 2 * sign_y)
                    for h in range(layout.halves):
                        lanes = slice(h * LANES, (h + 1) * LANES)
                        field_ref[cc, place, lanes] = sweep(parts[h], near[h], far[h], amount[:, lanes])
                return carry

            lax.fori_loop(0, run, component, 0, unroll=9)

        quadrant = (start % ND) // run
        for at, signs in enumerate(((1, 1), (-1, 1), (-1, -1), (1, -1))):
            pl.when(quadrant == at)(lambda signs=signs: run_all(*signs))

        def put(t, h, cc, value):
            out_ref[wire.lines(t, h, step * run + cc), :] = value

        def base_value(t, h, cc):
            value = view(field_ref.at[cc], layout.hosts[t], h)
            if packed:
                guest = view(field_ref.at[cc], *layout.guests[layout.guest_of(t, h)])
                value = jnp.where(view(sea_ref, layout.hosts[t], h) > 0.0, value, take_lanes(guest, view(fill_ref, t, h)))
            return value

        for b in wire.blocks:
            for cc in range(run):
                put(*layout.blocks[b], cc, base_value(*layout.blocks[b], cc))
        if not packed:
            return

        def fill_spare(b):
            t, h = layout.blocks[b]
            spare = view(spare_ref, t, h)
            for cc in range(run):
                value = base_value(t, h, cc)
                for j, guest in enumerate(layout.guests):
                    if j != layout.guest_of(t, h):
                        other = take_lanes(view(field_ref.at[cc], *guest), spare & (LANES - 1))
                        value = jnp.where(spare >> 7 == j, other, value)
                put(t, h, cc, value)

        @pl.when(flag_ref[len(layout.blocks)] > 0)
        def _():
            for b in wire.blocks:
                pl.when(flag_ref[b] >= 0)(lambda b=b: fill_spare(b))

    smem = pl.BlockSpec(memory_space=pltpu.SMEM)

    def fixed(array):
        return pl.BlockSpec(array.shape, lambda i: (0,) * array.ndim)

    extra_smem = [filling[2]] if packed else []
    extra = list(filling[:2]) if packed else []
    shape = (wire.groups * wire.pitch, LANES)
    out = pl.pallas_call(
        body,
        grid=(steps,),
        in_specs=[smem] * (3 + len(extra_smem)) + [pl.BlockSpec((run, rows, columns), lambda i: (i, 0, 0))] + [fixed(edge) for edge in edges] + [fixed(mask), fixed(depth_level)] + [fixed(a) for a in extra],
        out_specs=pl.BlockSpec(shape, lambda i: (0, 0)),
        out_shape=jax.ShapeDtypeStruct(shape, jnp.float32),
        scratch_shapes=[
            pltpu.VMEM((rows, columns), jnp.float32),
            pltpu.VMEM((rows, columns), jnp.float32),
            pltpu.VMEM((run, rows + 2 * SUBS, columns), jnp.float32),
            pltpu.VMEM((run, rows, columns), jnp.float32),
        ],
        compiler_params=pltpu.CompilerParams(vmem_limit_bytes=VMEM_LIMIT, dimension_semantics=("arbitrary",)),
        name="propagate",
    )((group_index * per_group).reshape(1), turns, speed_table.T, *extra_smem, spectrum, *edges, mask, depth_level, *extra)
    return out.reshape(wire.groups, wire.pitch, LANES)


def apply_source(wire, values, per_group, spot, east, north, turns, coupling):
    groups, pitch, even = wire.groups, wire.pitch, wire.even
    total = groups * per_group
    pairs = len(wire.tiles) // 2
    period = 2 * ND
    pieces = 9
    piece = total // pieces
    phase, weight, damping, by_direction = spectral_tables(period)

    def body(spot_ref, main_ref, last_ref, east_ref, north_ref, turn_ref, coupling_ref, dir_ref, out_ref,
             low_ref, high_ref, round_ref, wind_ref, mix_ref, stage_ref, rest_ref, sem):
        pair = pl.program_id(0)
        value_refs = (low_ref, high_ref)
        subrow = lax.broadcasted_iota(jnp.int32, (SUBS, LANES), 0)

        def constant(table, start):
            low, high = start // ND, (start + SUBS - 1) // ND
            if low == high:
                return float(table[low])
            return jnp.where(subrow < high * ND - start, float(table[low]), float(table[high]))

        def line(ref, half):
            tile = ref[pl.ds(pl.multiple_of((2 * pair + half) * SUBS, SUBS), SUBS), :]
            tile = jnp.where(spot_ref[1] == 0, tile[:, :LANES], tile[:, LANES:])
            row = jnp.sum(jnp.where(subrow == spot_ref[0], tile, 0.0), axis=0, keepdims=True)
            return jnp.broadcast_to(row, (SUBS, LANES))

        @pl.when(pair == 0)
        def _():
            for k in range(groups):
                rest_ref[pl.ds(k * SUBS, SUBS), :] = last_ref[k]

        turn_line = [line(turn_ref, half) for half in range(2)]
        step_line = [TIME_STEP / t for t in turn_line]
        for half, ref in enumerate(value_refs):
            for k in range(groups):
                ref[pl.ds(k * per_group, even), :] = main_ref[k, pl.ds(half * even, even), :]
            ref[pl.ds(even, groups, stride=per_group), :] = rest_ref[pl.ds(2 * pair + half, groups, stride=SUBS), :]
            east_line, north_line = line(east_ref, half), line(north_ref, half)
            for i in range(0, period, SUBS):
                columns = dir_ref[pl.ds(i, SUBS), :]
                wind_ref[pl.ds(i, SUBS), pl.ds(half * LANES, LANES)] = east_line * columns[:, 0:1] + north_line * columns[:, 1:2]

        def sweep(change):
            squares = []
            for half, ref in enumerate(value_refs):
                steep = jnp.zeros((SUBS, LANES), jnp.float32)
                for f in range(0, NF, 2):
                    sums = [None, None]
                    for start in range(f * ND, (f + 2) * ND, SUBS):
                        place = pl.ds(start, SUBS)
                        value = ref[place, :]
                        if change is not None:
                            value = change(half, start, value)
                            ref[place, :] = value
                        low, high = start // ND, (start + SUBS - 1) // ND
                        if low != high:
                            steep = steep + constant(weight, start) * value
                        else:
                            sums[low - f] = value if sums[low - f] is None else sums[low - f] + value
                    steep = steep + float(weight[f]) * sums[0] + float(weight[f + 1]) * sums[1]
                steepness = jnp.broadcast_to(jnp.sum(steep, axis=0, keepdims=True), (SUBS, LANES))
                squares.append(steepness * steepness)
            return tuple(squares)

        def round_all():
            for half, ref in enumerate(value_refs):
                for start in range(0, total, 2 * SUBS):
                    place = pl.ds(start, 2 * SUBS)
                    round_ref[place, pl.ds(half * LANES, LANES)] = ref[place, :].astype(jnp.bfloat16)

        def turn(repeat, squares):
            for i in range(pieces):
                place = pl.ds(i * piece, piece)
                mix_ref[place, :] = jnp.dot(coupling_ref[place, :], round_ref[...], preferred_element_type=jnp.float32)

            def change(half, start, value):
                lanes = pl.ds(half * LANES, LANES)
                rate = jnp.maximum(0.0, wind_ref[pl.ds(start % period, SUBS), lanes] - constant(phase, start))
                rate = rate - constant(damping, start) * squares[half]
                step = step_line[half]
                moved = value + step * (rate * value + MIXING * mix_ref[pl.ds(start, SUBS), lanes])
                return jnp.where(repeat.astype(jnp.float32) < turn_line[half], moved, value)

            squares = sweep(change)
            round_all()
            return squares

        squares = sweep(None)
        round_all()
        most = jnp.max(jnp.maximum(turn_line[0], turn_line[1])).astype(jnp.int32)
        lax.fori_loop(0, most, turn, squares)

        for half, ref in enumerate(value_refs):
            for k in range(groups):
                stage_ref[pair, k, pl.ds(half * even, even), :] = ref[pl.ds(k * per_group, even), :]
            rest_ref[pl.ds(2 * pair + half, groups, stride=SUBS), :] = ref[pl.ds(even, groups, stride=per_group), :]

        def send(p):
            return pltpu.make_async_copy(stage_ref.at[p], out_ref.at[:, pl.ds(p * 2 * even, 2 * even), :], sem.at[p])

        send(pair).start()

        @pl.when(pair == pairs - 1)
        def _():
            final = [
                pltpu.make_async_copy(rest_ref.at[pl.ds(k * SUBS, SUBS)], out_ref.at[k, pl.ds(pitch - SUBS, SUBS), :], sem.at[pairs + k])
                for k in range(groups)
            ]
            for copy in final:
                copy.start()
            for copy in final:
                copy.wait()
            for p in range(pairs):
                send(p).wait()

    def fixed(array):
        return pl.BlockSpec(array.shape, lambda i: (0,) * array.ndim)

    return pl.pallas_call(
        body,
        grid=(pairs,),
        in_specs=[
            SMEM_SPEC,
            pl.BlockSpec((groups, 2 * even, LANES), lambda i: (0, i, 0)),
            pl.BlockSpec((groups, SUBS, LANES), lambda i: (0, pitch // SUBS - 1, 0)),
        ]
        + [fixed(array) for array in (east, north, turns, coupling, by_direction)],
        out_specs=pl.BlockSpec(memory_space=pl.ANY),
        out_shape=jax.ShapeDtypeStruct((groups, pitch, LANES), jnp.float32),
        scratch_shapes=[
            pltpu.VMEM((total, LANES), jnp.float32),
            pltpu.VMEM((total, LANES), jnp.float32),
            pltpu.VMEM((total, 2 * LANES), jnp.bfloat16),
            pltpu.VMEM((period, 2 * LANES), jnp.float32),
            pltpu.VMEM((total, 2 * LANES), jnp.float32),
            pltpu.VMEM((pairs, groups, 2 * even, LANES), jnp.float32),
            pltpu.VMEM((groups * SUBS, LANES), jnp.float32),
            pltpu.SemaphoreType.DMA((pairs + groups,)),
        ],
        compiler_params=pltpu.CompilerParams(vmem_limit_bytes=VMEM_LIMIT, dimension_semantics=("arbitrary",)),
        name="source",
    )(spot, values, values, east, north, turns, coupling, by_direction)


def unpack(layout, wires, arrays, per_group, mask, back):
    run = ND // 4
    steps = per_group // run
    rows, columns = mask.shape
    packed = len(layout.guests) > 0

    def body(*refs):
        refs = list(refs)
        flag_ref = refs.pop(0) if packed else None
        wire_refs = [refs.pop(0) for _ in wires]
        mask_ref = refs.pop(0)
        back_ref = refs.pop(0) if packed else None
        target_ref, held_ref, sem = refs
        step = pl.program_id(0)
        out_ref = held_ref.at[pl.ds(step * run, run)]

        def get(t, h, cc):
            for wire, ref in zip(wires, wire_refs):
                if t in wire.tiles:
                    return ref[wire.lines(t, h, step * run + cc), :]

        def fetch(j, blocks):
            t, h = layout.guests[j]
            place = (pl.ds(t * SUBS, SUBS), pl.ds(h * LANES, LANES))
            back = view(back_ref, layout.guest_tiles.index(t), h)
            for cc in range(run):
                value = jnp.zeros((SUBS, LANES), jnp.float32)
                for b in blocks:
                    found = take_lanes(get(*layout.blocks[b], cc), back & (LANES - 1))
                    value = jnp.where(back >> 7 == b, found, value)
                out_ref[(cc,) + place] = value

        for i, h in layout.blocks:
            place = (pl.ds(layout.hosts[i] * SUBS, SUBS), pl.ds(h * LANES, LANES))
            sea = mask_ref[place] > 0
            for cc in range(run):
                out_ref[(cc,) + place] = jnp.where(sea, get(i, h, cc), 0.0)
        for j in range(len(layout.guests)):
            fetch(j, [b for b, at in enumerate(layout.blocks) if layout.guest_of(*at) == j])
        for j in range(len(layout.guests)):
            pl.when(flag_ref[j] != 0)(lambda j=j: fetch(j, range(len(layout.blocks))))

        def send(at):
            place = pl.ds(at * run, run)
            return pltpu.make_async_copy(held_ref.at[place], target_ref.at[place], sem.at[at])

        send(step).start()

        @pl.when(step == steps - 1)
        def _():
            for at in range(steps):
                send(at).wait()

    smem = pl.BlockSpec(memory_space=pltpu.SMEM)
    extra_smem = [back[1]] if packed else []
    inputs = [array.reshape(-1, LANES) for array in arrays] + [mask] + ([back[0]] if packed else [])
    return pl.pallas_call(
        body,
        grid=(steps,),
        in_specs=[smem] * len(extra_smem) + [pl.BlockSpec(a.shape, lambda i: (0, 0)) for a in inputs],
        out_specs=pl.BlockSpec(memory_space=pltpu.HBM),
        out_shape=pltpu.HBM((per_group, rows, columns), jnp.float32),
        scratch_shapes=[pltpu.VMEM((per_group, rows, columns), jnp.float32), pltpu.SemaphoreType.DMA((steps,))],
        compiler_params=pltpu.CompilerParams(vmem_limit_bytes=VMEM_LIMIT, dimension_semantics=("arbitrary",)),
        name="unpack",
    )(*extra_smem, *inputs)


def regroup(wire):
    return lax.all_to_all(wire, "comp", split_axis=0, concat_axis=0, tiled=True)


def on_device(spectrum, mask, depth_level, speed_table, wind_u, wind_v, substeps, coupling):
    per_group, rows, columns = spectrum.shape
    group_index = lax.axis_index("comp")
    tiles = rows // SUBS
    edges = jnp.concatenate([spectrum[:, :2], spectrum[:, -2:]], axis=1) * jnp.concatenate([mask[:2], mask[-2:]], axis=0).astype(jnp.float32)[None]
    edges = edge_rows(edges, "space", 2)
    spot = jnp.stack([group_index % SUBS, group_index // SUBS])
    guests = [tiles // 2 - 1, tiles // 2]
    hosts = [t for t in range(tiles) if t not in guests]

    def step(hosts, guests, filling, east, north, turns, back):
        layout = Layout(rows, columns, hosts, guests)
        wire = Wire(layout, per_group, range(len(hosts)))
        values = regroup(propagate(layout, wire, spectrum, edges, mask, depth_level, speed_table, group_index, filling))
        values = regroup(apply_source(wire, values, per_group, spot, east, north, turns, coupling))
        return unpack(layout, [wire], [values], per_group, mask, back)

    fill, spare, back, east, north, turns, flag, back_flag, fits = make_plan(
        Layout(rows, columns, hosts, guests), mask, wind_u, wind_v, substeps
    )
    every = jnp.broadcast_to(substeps.astype(jnp.float32)[:, None], mask.shape)
    return lax.cond(
        fits[0] > 0,
        lambda: step(hosts, guests, (fill, spare, flag), east, north, turns, (back, back_flag)),
        lambda: step(list(range(tiles)), [], None, wind_u, wind_v, every, None),
    )


def solution(mesh):
    placed = (
        P("comp", "space", None),
        P("space", None),
        P("space", None),
        P(),
        P("space", None),
        P("space", None),
        P("space"),
        P(),
    )
    return jax.shard_map(
        on_device, mesh=mesh, in_specs=placed, out_specs=P("comp", "space", None), check_vma=False
    )
```

```python
import math

import jax
import jax.numpy as jnp
import numpy as np
from jax import lax
from jax.experimental import pallas as pl
from jax.experimental.pallas import tpu as pltpu
from jax.sharding import PartitionSpec as P

NF = 36
ND = 36
LEVELS = 8

TIME_STEP = 1.0
WIND_RATE = 0.3
BREAK_RATE = 0.8
MIXING = 0.5

LANES = 128
SUBS = 8
MIB = 1024 * 1024


def edge_rows(cells, axis, width):
    count = lax.axis_size(axis)
    ends = count - 1
    head = cells[:, :width]
    tail = cells[:, -width:]
    below = lax.ppermute(tail, axis, [(i, i + 1) for i in range(ends)])
    above = lax.ppermute(head, axis, [(i + 1, i) for i in range(ends)])
    return below, above


def spectral_tables(period):
    frequency = np.arange(NF, dtype=np.float64)
    angle = 2.0 * math.pi / ND * (np.arange(ND) + 0.5)
    norm_total = ND * np.sum(np.power(1.1, 2.0 * frequency))
    phase = WIND_RATE * 1.5 * np.power(1.1, -frequency)
    weight = np.power(1.1, 2.0 * frequency) / norm_total
    damping = BREAK_RATE * (frequency + 1.0) / NF
    by_direction = np.zeros((period, SUBS))
    by_direction[:, 0] = WIND_RATE * np.tile(np.cos(angle), period // ND)
    by_direction[:, 1] = WIND_RATE * np.tile(np.sin(angle), period // ND)
    return phase, weight, damping, jnp.asarray(by_direction.astype(np.float32))


def take_lanes(values, index):
    return jnp.take_along_axis(values, index, axis=1, mode="promise_in_bounds")


class Layout:
    def __init__(self, rows, columns, hosts, guests):
        self.tiles = rows // SUBS
        self.halves = columns // LANES
        self.hosts = hosts
        self.guest_tiles = guests
        self.guests = [(t, h) for t in guests for h in range(self.halves)]
        self.blocks = [(i, h) for i in range(len(hosts)) for h in range(self.halves)]
        self.share = len(hosts) // len(guests) if guests else 0

    def guest_of(self, i, h):
        return (i // self.share) * self.halves + h


def view(ref, t, h):
    return ref[pl.ds(t * SUBS, SUBS), pl.ds(h * LANES, LANES)]


def count_blocks(layout, mask_ref):
    marked = [1 - view(mask_ref, layout.hosts[i], h) for i, h in layout.blocks]
    marked = jnp.concatenate(marked + [view(mask_ref, t, h) for t, h in layout.guests], axis=0)
    lane = lax.broadcasted_iota(jnp.int32, marked.shape, 1)
    upto = (lax.broadcasted_iota(jnp.int32, (LANES, LANES), 0) <= lax.broadcasted_iota(jnp.int32, (LANES, LANES), 1)).astype(jnp.bfloat16)
    total = jnp.dot(marked.astype(jnp.bfloat16), upto, preferred_element_type=jnp.float32).astype(jnp.int32)
    rank = total - marked
    state = jnp.where(marked > 0, lane + LANES * (lane - rank), -1)
    for bit in range(7):
        moved = pltpu.roll(state, LANES - (1 << bit), 1)
        take = (moved >= 0) & (((moved >> (7 + bit)) & 1) == 1)
        stay = (state >= 0) & (((state >> (7 + bit)) & 1) == 0)
        state = jnp.where(take, moved, jnp.where(stay, state, -1))
    place = jnp.maximum(state, 0) & (LANES - 1)
    count = jnp.broadcast_to(total[:, LANES - 1:], marked.shape)

    def parts(array):
        each = [array[i:i + SUBS] for i in range(0, array.shape[0], SUBS)]
        return each[:len(layout.blocks)], each[len(layout.blocks):]

    return parts(marked), parts(rank), parts(place), parts(count)


class Plan:
    def __init__(self, layout, mask_ref):
        (hole, self.sea), (self.hole_rank, self.sea_rank), (self.hole_at, self.sea_at), counts = count_blocks(layout, mask_ref)
        self.hole_count, self.sea_count = counts
        self.hole = [m > 0 for m in hole]
        self.sea = [m > 0 for m in self.sea]
        guests = len(layout.guests)
        zero = jnp.zeros((SUBS, LANES), jnp.int32)
        self.start = []
        self.holes_of = [zero] * guests
        for b, at in enumerate(layout.blocks):
            j = layout.guest_of(*at)
            self.start.append(self.holes_of[j])
            self.holes_of[j] = self.holes_of[j] + self.hole_count[b]
        self.open_of = [jnp.maximum(self.holes_of[j] - self.sea_count[j], 0) for j in range(guests)]
        self.left_of = [jnp.maximum(self.sea_count[j] - self.holes_of[j], 0) for j in range(guests)]
        self.open_start, self.left_start = [zero], [zero]
        for j in range(1, guests):
            self.open_start.append(self.open_start[-1] + self.open_of[j - 1])
            self.left_start.append(self.left_start[-1] + self.left_of[j - 1])


def inside(index):
    return jnp.clip(index, 0, LANES - 1)


VMEM_SPEC = pl.BlockSpec(memory_space=pltpu.VMEM)
SMEM_SPEC = pl.BlockSpec(memory_space=pltpu.SMEM)


def make_plan(layout, mask, wind_u, wind_v, substeps):
    columns = mask.shape[1]

    def body(mask_ref, u_ref, v_ref, n_ref, fill_ref, spare_ref, back_ref, uo_ref, vo_ref, no_ref, flag_ref, back_flag, fits_ref):
        p = Plan(layout, mask_ref)
        subrow = lax.broadcasted_iota(jnp.int32, (SUBS, LANES), 0)
        ranks = []

        def turns_of(t):
            result = jnp.zeros((SUBS, LANES), jnp.int32)
            for r in range(SUBS):
                result = jnp.where(subrow == r, n_ref[t * SUBS + r], result)
            return result.astype(jnp.float32)

        every = {t: turns_of(t) for t in range(layout.tiles)}
        for b, (i, h) in enumerate(layout.blocks):
            own = layout.guest_of(i, h)
            rank = p.start[b] + p.hole_rank[b]
            ranks.append(rank)
            first = take_lanes(p.sea_at[own], inside(rank))
            place = (pl.ds(i * SUBS, SUBS), pl.ds(h * LANES, LANES))
            fill_ref[place] = first
            flag_ref[b] = -1
            hole = p.hole[b]
            for source, target in ((u_ref, uo_ref), (v_ref, vo_ref)):
                value = take_lanes(view(source, *layout.guests[own]), first)
                target[place] = jnp.where(hole, value, view(source, layout.hosts[i], h))
            guest = jnp.where(rank < p.sea_count[own], every[layout.guests[own][0]], 1.0)
            no_ref[place] = jnp.where(hole, guest, every[layout.hosts[i]])

        for j, (t, h) in enumerate(layout.guests):
            rank = p.sea_rank[j]
            back = jnp.full((SUBS, LANES), -1, jnp.int32)
            for b, block in enumerate(layout.blocks):
                if layout.guest_of(*block) == j:
                    ok = p.sea[j] & (rank >= p.start[b]) & (rank < p.start[b] + p.hole_count[b])
                    back = jnp.where(ok, LANES * b + take_lanes(p.hole_at[b], inside(rank - p.start[b])), back)
            back_ref[pl.ds(layout.guest_tiles.index(t) * SUBS, SUBS), pl.ds(h * LANES, LANES)] = back
            back_flag[j] = 0

        left = sum(p.left_of)
        flag_ref[len(layout.blocks)] = jnp.max(left)
        fits_ref[0] = (jnp.max(left - sum(p.open_of)) <= 0).astype(jnp.int32)

        @pl.when(jnp.max(left) > 0)
        def _():
            spare_ref[...] = jnp.full(spare_ref.shape, -1, jnp.int32)
            for j, guest in enumerate(layout.guests):
                @pl.when(jnp.max(p.left_of[j]) > 0)
                def _():
                    for b, (i, h) in enumerate(layout.blocks):
                        own = layout.guest_of(i, h)
                        if own == j:
                            continue
                        extra = p.open_start[own] + ranks[b] - p.sea_count[own] - p.left_start[j]
                        ok = p.hole[b] & (ranks[b] >= p.sea_count[own]) & (extra >= 0) & (extra < p.left_of[j])
                        found = take_lanes(p.sea_at[j], inside(extra + p.holes_of[j]))
                        place = (pl.ds(i * SUBS, SUBS), pl.ds(h * LANES, LANES))
                        spare_ref[place] = jnp.where(ok, LANES * j + found, spare_ref[place])
                        for source, target in ((u_ref, uo_ref), (v_ref, vo_ref)):
                            target[place] = jnp.where(ok, take_lanes(view(source, *guest), found), target[place])
                        no_ref[place] = jnp.where(ok, every[guest[0]], no_ref[place])
            for b, (i, h) in enumerate(layout.blocks):
                flag_ref[b] = jnp.max(view(spare_ref, i, h))

            for j, (t, h) in enumerate(layout.guests):
                @pl.when(jnp.max(p.left_of[j]) > 0)
                def _():
                    place = (pl.ds(layout.guest_tiles.index(t) * SUBS, SUBS), pl.ds(h * LANES, LANES))
                    back = back_ref[place]
                    rank = p.sea_rank[j]
                    extra = p.left_start[j] + rank - p.holes_of[j]
                    for b, block in enumerate(layout.blocks):
                        own = layout.guest_of(*block)
                        if own != j:
                            at = extra - p.open_start[own] + p.sea_count[own]
                            ok = p.sea[j] & (rank >= p.holes_of[j])
                            ok = ok & (extra >= p.open_start[own]) & (extra < p.open_start[own] + p.open_of[own])
                            ok = ok & (at >= p.start[b]) & (at < p.start[b] + p.hole_count[b])
                            back = jnp.where(ok, LANES * b + take_lanes(p.hole_at[b], inside(at - p.start[b])), back)
                    back_ref[place] = back
                    back_flag[j] = 1

    whole = (len(layout.hosts) * SUBS, columns)
    return pl.pallas_call(
        body,
        in_specs=[VMEM_SPEC] * 3 + [SMEM_SPEC],
        out_specs=[VMEM_SPEC] * 6 + [SMEM_SPEC] * 3,
        out_shape=[
            jax.ShapeDtypeStruct(whole, jnp.int32),
            jax.ShapeDtypeStruct(whole, jnp.int32),
            jax.ShapeDtypeStruct((len(layout.guest_tiles) * SUBS, columns), jnp.int32),
            jax.ShapeDtypeStruct(whole, jnp.float32),
            jax.ShapeDtypeStruct(whole, jnp.float32),
            jax.ShapeDtypeStruct(whole, jnp.float32),
            jax.ShapeDtypeStruct((len(layout.blocks) + 1,), jnp.int32),
            jax.ShapeDtypeStruct((len(layout.guests),), jnp.int32),
            jax.ShapeDtypeStruct((1,), jnp.int32),
        ],
        name="plan",
    )(mask, wind_u, wind_v, substeps)


class Wire:
    def __init__(self, layout, per_group, tiles):
        self.tiles = tiles
        self.even = per_group // SUBS * SUBS
        self.rest = per_group - self.even
        self.rest_start = len(tiles) * self.even
        self.pitch = -(-(len(tiles) * per_group) // SUBS) * SUBS
        self.groups = SUBS * layout.halves
        self.blocks = [b for b, (i, h) in enumerate(layout.blocks) if i in tiles]

    def row(self, t, c):
        t = t - self.tiles[0]
        return jnp.where(c < self.even, t * self.even + c, self.rest_start + t * self.rest + c - self.even)

    def lines(self, t, h, c):
        return pl.ds(h * SUBS * self.pitch + self.row(t, c), SUBS, stride=self.pitch)


def propagate(layout, wire, spectrum, edges, mask, depth_level, speed_table, group_index, filling):
    per_group, rows, columns = spectrum.shape
    run = ND // 4
    steps = per_group // run
    angle = 2.0 * math.pi / ND * (np.arange(ND) + 0.5)
    turns = jnp.asarray(np.abs(np.stack([np.cos(angle), np.sin(angle)])).astype(np.float32))
    packed = len(layout.guests) > 0
    tiles = sorted([layout.hosts[i] for i in wire.tiles] + layout.guest_tiles)
    edged = len(edges) > 0

    def body(*refs):
        refs = list(refs)
        first_ref, turn_ref, speed_ref = refs[:3]
        flag_ref = refs[3] if packed else None
        refs = refs[3 + packed:]
        spec_ref = refs[0]
        below_ref, above_ref = refs[1:3] if edged else (None, None)
        refs = refs[1 + 2 * edged:]
        mask_ref, depth_ref = refs[:2]
        fill_ref, spare_ref = refs[2:4] if packed else (None, None)
        out_ref, base_ref, sea_ref, pad_ref, field_ref = refs[2 + 2 * packed:]
        step = pl.program_id(0)
        start = first_ref[0] + step * run
        f = start // ND

        @pl.when(step == 0)
        def _():
            sea_ref[...] = mask_ref[...].astype(jnp.float32)

        @pl.when((step == 0) | (start % ND == 0))
        def _():
            for t in tiles:
                place = pl.ds(t * SUBS, SUBS)
                level = depth_ref[place, :]
                speed = jnp.zeros(level.shape, jnp.float32)
                for l in range(LEVELS):
                    speed = jnp.where(level == l, speed_ref[l, f], speed)
                base_ref[place, :] = speed

        lane = lax.broadcasted_iota(jnp.int32, (SUBS, LANES), 1)

        def sweep(centre, near, far, amount):
            one = amount * (2.0 - amount)
            two = 0.5 * (amount - one)
            return centre + one * (near - centre) + two * (far - centre)

        def shifted(parts, by):
            turned = [pltpu.roll(part, by % LANES, 1) for part in parts]
            edge = jnp.zeros_like(turned[0])
            if by > 0:
                return [jnp.where(lane >= by, turned[i], turned[i - 1] if i else edge) for i in range(len(parts))]
            ends = turned[1:] + [edge]
            return [jnp.where(lane < LANES + by, turned[i], ends[i]) for i in range(len(parts))]

        def run_all(sign_x, sign_y):
            def component(cc, carry):
                d = start % ND + cc
                wide_x = turn_ref[0, d]
                wide_y = turn_ref[1, d]
                needed = sorted({n for t in tiles for n in (t, t - sign_x) if 0 <= n < layout.tiles})
                if edged:
                    pad_ref[cc, pl.ds(SUBS - 2, 2), :] = below_ref[step * run + cc]
                    pad_ref[cc, pl.ds(rows + SUBS, 2), :] = above_ref[step * run + cc]
                for t in needed:
                    place = pl.ds(t * SUBS, SUBS)
                    pad_ref[cc, pl.ds((t + 1) * SUBS, SUBS), :] = spec_ref[cc, place, :] * sea_ref[place, :]
                for t in tiles:
                    place = pl.ds(t * SUBS, SUBS)
                    at = (t + 1) * SUBS
                    base = base_ref[place, :]
                    centre = pad_ref[cc, pl.ds(at, SUBS), :]
                    near = pad_ref[cc, pl.ds(at - sign_x, SUBS), :]
                    far = pad_ref[cc, pl.ds(at - 2 * sign_x, SUBS), :]
                    centre = sweep(centre, near, far, base * wide_x) * sea_ref[place, :]
                    amount = base * wide_y
                    parts = [centre[:, h * LANES:(h + 1) * LANES] for h in range(layout.halves)]
                    near = shifted(parts, sign_y)
                    far = shifted(parts, 2 * sign_y)
                    for h in range(layout.halves):
                        lanes = slice(h * LANES, (h + 1) * LANES)
                        field_ref[cc, place, lanes] = sweep(parts[h], near[h], far[h], amount[:, lanes])
                return carry

            lax.fori_loop(0, run, component, 0, unroll=9)

        quadrant = (start % ND) // run
        for at, signs in enumerate(((1, 1), (-1, 1), (-1, -1), (1, -1))):
            pl.when(quadrant == at)(lambda signs=signs: run_all(*signs))

        def put(t, h, cc, value):
            out_ref[wire.lines(t, h, step * run + cc), :] = value

        def base_value(t, h, cc):
            value = view(field_ref.at[cc], layout.hosts[t], h)
            if packed:
                guest = view(field_ref.at[cc], *layout.guests[layout.guest_of(t, h)])
                value = jnp.where(view(sea_ref, layout.hosts[t], h) > 0.0, value, take_lanes(guest, view(fill_ref, t, h)))
            return value

        for b in wire.blocks:
            for cc in range(run):
                put(*layout.blocks[b], cc, base_value(*layout.blocks[b], cc))
        if not packed:
            return

        def fill_spare(b):
            t, h = layout.blocks[b]
            spare = view(spare_ref, t, h)
            for cc in range(run):
                value = base_value(t, h, cc)
                for j, guest in enumerate(layout.guests):
                    if j != layout.guest_of(t, h):
                        other = take_lanes(view(field_ref.at[cc], *guest), spare & (LANES - 1))
                        value = jnp.where(spare >> 7 == j, other, value)
                put(t, h, cc, value)

        @pl.when(flag_ref[len(layout.blocks)] > 0)
        def _():
            for b in wire.blocks:
                pl.when(flag_ref[b] >= 0)(lambda b=b: fill_spare(b))

    smem = pl.BlockSpec(memory_space=pltpu.SMEM)

    def fixed(array):
        return pl.BlockSpec(array.shape, lambda i: (0,) * array.ndim)

    extra_smem = [filling[2]] if packed else []
    extra = list(filling[:2]) if packed else []
    shape = (wire.groups * wire.pitch, LANES)
    out = pl.pallas_call(
        body,
        grid=(steps,),
        in_specs=[smem] * (3 + len(extra_smem)) + [pl.BlockSpec((run, rows, columns), lambda i: (i, 0, 0))] + [fixed(edge) for edge in edges] + [fixed(mask), fixed(depth_level)] + [fixed(a) for a in extra],
        out_specs=VMEM_SPEC,
        out_shape=jax.ShapeDtypeStruct(shape, jnp.float32),
        scratch_shapes=[
            pltpu.VMEM((rows, columns), jnp.float32),
            pltpu.VMEM((rows, columns), jnp.float32),
            pltpu.VMEM((run, rows + 2 * SUBS, columns), jnp.float32),
            pltpu.VMEM((run, rows, columns), jnp.float32),
        ],
        compiler_params=pltpu.CompilerParams(vmem_limit_bytes=24 * MIB, dimension_semantics=("arbitrary",)),
        name="propagate",
    )((group_index * per_group).reshape(1), turns, speed_table.T, *extra_smem, spectrum, *edges, mask, depth_level, *extra)
    return out.reshape(wire.groups, wire.pitch, LANES)


def apply_source(wire, values, per_group, spot, east, north, turns, coupling):
    groups, pitch, even = wire.groups, wire.pitch, wire.even
    total = groups * per_group
    pairs = len(wire.tiles) // 2
    period = 2 * ND
    pieces = 9
    piece = total // pieces
    phase, weight, damping, by_direction = spectral_tables(period)

    def body(spot_ref, wire_ref, east_ref, north_ref, turn_ref, coupling_ref, dir_ref, out_ref,
             low_ref, high_ref, round_ref, wind_ref, mix_ref, rest_ref):
        pair = pl.program_id(0)
        value_refs = (low_ref, high_ref)
        subrow = lax.broadcasted_iota(jnp.int32, (SUBS, LANES), 0)

        def constant(table, start):
            low, high = start // ND, (start + SUBS - 1) // ND
            if low == high:
                return float(table[low])
            return jnp.where(subrow < high * ND - start, float(table[low]), float(table[high]))

        def line(ref, half):
            tile = ref[pl.ds(pl.multiple_of((2 * pair + half) * SUBS, SUBS), SUBS), :]
            tile = jnp.where(spot_ref[1] == 0, tile[:, :LANES], tile[:, LANES:])
            row = jnp.sum(jnp.where(subrow == spot_ref[0], tile, 0.0), axis=0, keepdims=True)
            return jnp.broadcast_to(row, (SUBS, LANES))

        @pl.when(pair == 0)
        def _():
            for k in range(groups):
                rest_ref[pl.ds(k * SUBS, SUBS), :] = wire_ref[k, pl.ds(pitch - SUBS, SUBS), :]

        def rows_of(half):
            return pl.ds(pl.multiple_of((2 * pair + half) * even, SUBS), even)

        turn_line = [line(turn_ref, half) for half in range(2)]
        step_line = [TIME_STEP / t for t in turn_line]
        for half, ref in enumerate(value_refs):
            for k in range(groups):
                ref[pl.ds(k * per_group, even), :] = wire_ref[k, rows_of(half), :]
            ref[pl.ds(even, groups, stride=per_group), :] = rest_ref[pl.ds(2 * pair + half, groups, stride=SUBS), :]
            east_line, north_line = line(east_ref, half), line(north_ref, half)
            for i in range(0, period, SUBS):
                columns = dir_ref[pl.ds(i, SUBS), :]
                wind_ref[pl.ds(i, SUBS), pl.ds(half * LANES, LANES)] = east_line * columns[:, 0:1] + north_line * columns[:, 1:2]

        def sweep(change):
            squares = []
            for half, ref in enumerate(value_refs):
                steep = jnp.zeros((SUBS, LANES), jnp.float32)
                for f in range(0, NF, 2):
                    sums = [None, None]
                    for start in range(f * ND, (f + 2) * ND, SUBS):
                        place = pl.ds(start, SUBS)
                        value = ref[place, :]
                        if change is not None:
                            value = change(half, start, value)
                            ref[place, :] = value
                        low, high = start // ND, (start + SUBS - 1) // ND
                        if low != high:
                            steep = steep + constant(weight, start) * value
                        else:
                            sums[low - f] = value if sums[low - f] is None else sums[low - f] + value
                    steep = steep + float(weight[f]) * sums[0] + float(weight[f + 1]) * sums[1]
                steepness = jnp.broadcast_to(jnp.sum(steep, axis=0, keepdims=True), (SUBS, LANES))
                squares.append(steepness * steepness)
            return tuple(squares)

        def round_all():
            for half, ref in enumerate(value_refs):
                for start in range(0, total, 2 * SUBS):
                    place = pl.ds(start, 2 * SUBS)
                    round_ref[place, pl.ds(half * LANES, LANES)] = ref[place, :].astype(jnp.bfloat16)

        def turn(repeat, squares):
            for i in range(pieces):
                place = pl.ds(i * piece, piece)
                mix_ref[place, :] = jnp.dot(coupling_ref[place, :], round_ref[...], preferred_element_type=jnp.float32)

            def change(half, start, value):
                lanes = pl.ds(half * LANES, LANES)
                rate = jnp.maximum(0.0, wind_ref[pl.ds(start % period, SUBS), lanes] - constant(phase, start))
                rate = rate - constant(damping, start) * squares[half]
                step = step_line[half]
                moved = value + step * (rate * value + MIXING * mix_ref[pl.ds(start, SUBS), lanes])
                return jnp.where(repeat.astype(jnp.float32) < turn_line[half], moved, value)

            squares = sweep(change)
            round_all()
            return squares

        squares = sweep(None)
        round_all()
        most = jnp.max(jnp.maximum(turn_line[0], turn_line[1])).astype(jnp.int32)
        lax.fori_loop(0, most, turn, squares)

        for half, ref in enumerate(value_refs):
            for k in range(groups):
                out_ref[k, rows_of(half), :] = ref[pl.ds(k * per_group, even), :]
            rest_ref[pl.ds(2 * pair + half, groups, stride=SUBS), :] = ref[pl.ds(even, groups, stride=per_group), :]

        @pl.when(pair == pairs - 1)
        def _():
            for k in range(groups):
                out_ref[k, pl.ds(pitch - SUBS, SUBS), :] = rest_ref[pl.ds(k * SUBS, SUBS), :]

    return pl.pallas_call(
        body,
        grid=(pairs,),
        in_specs=[SMEM_SPEC] + [VMEM_SPEC] * 6,
        out_specs=VMEM_SPEC,
        out_shape=jax.ShapeDtypeStruct((groups, pitch, LANES), jnp.float32),
        scratch_shapes=[
            pltpu.VMEM((total, LANES), jnp.float32),
            pltpu.VMEM((total, LANES), jnp.float32),
            pltpu.VMEM((total, 2 * LANES), jnp.bfloat16),
            pltpu.VMEM((period, 2 * LANES), jnp.float32),
            pltpu.VMEM((total, 2 * LANES), jnp.float32),
            pltpu.VMEM((groups * SUBS, LANES), jnp.float32),
        ],
        compiler_params=pltpu.CompilerParams(vmem_limit_bytes=32 * MIB, dimension_semantics=("arbitrary",)),
        name="source",
    )(spot, values, east, north, turns, coupling, by_direction)


def unpack(layout, wires, arrays, per_group, mask, back):
    run = ND // 4
    steps = per_group // run
    rows, columns = mask.shape
    packed = len(layout.guests) > 0

    def body(*refs):
        refs = list(refs)
        flag_ref = refs.pop(0) if packed else None
        wire_refs = [refs.pop(0) for _ in wires]
        mask_ref = refs.pop(0)
        back_ref = refs.pop(0) if packed else None
        target_ref, held_ref, sem = refs
        step = pl.program_id(0)
        out_ref = held_ref.at[pl.ds(step * run, run)]

        def get(t, h, cc):
            for wire, ref in zip(wires, wire_refs):
                if t in wire.tiles:
                    return ref[wire.lines(t, h, step * run + cc), :]

        def fetch(j, blocks):
            t, h = layout.guests[j]
            place = (pl.ds(t * SUBS, SUBS), pl.ds(h * LANES, LANES))
            back = view(back_ref, layout.guest_tiles.index(t), h)
            for cc in range(run):
                value = jnp.zeros((SUBS, LANES), jnp.float32)
                for b in blocks:
                    found = take_lanes(get(*layout.blocks[b], cc), back & (LANES - 1))
                    value = jnp.where(back >> 7 == b, found, value)
                out_ref[(cc,) + place] = value

        for i, h in layout.blocks:
            place = (pl.ds(layout.hosts[i] * SUBS, SUBS), pl.ds(h * LANES, LANES))
            sea = mask_ref[place] > 0
            for cc in range(run):
                out_ref[(cc,) + place] = jnp.where(sea, get(i, h, cc), 0.0)
        for j in range(len(layout.guests)):
            fetch(j, [b for b, at in enumerate(layout.blocks) if layout.guest_of(*at) == j])
        for j in range(len(layout.guests)):
            pl.when(flag_ref[j] != 0)(lambda j=j: fetch(j, range(len(layout.blocks))))

        def send(at):
            place = pl.ds(at * run, run)
            return pltpu.make_async_copy(held_ref.at[place], target_ref.at[place], sem.at[at])

        send(step).start()

        @pl.when(step == steps - 1)
        def _():
            for at in range(steps):
                send(at).wait()

    smem = pl.BlockSpec(memory_space=pltpu.SMEM)
    extra_smem = [back[1]] if packed else []
    inputs = [array.reshape(-1, LANES) for array in arrays] + [mask] + ([back[0]] if packed else [])
    return pl.pallas_call(
        body,
        grid=(steps,),
        in_specs=[smem] * len(extra_smem) + [VMEM_SPEC] * len(inputs),
        out_specs=pl.BlockSpec(memory_space=pltpu.HBM),
        out_shape=pltpu.HBM((per_group, rows, columns), jnp.float32),
        scratch_shapes=[pltpu.VMEM((per_group, rows, columns), jnp.float32), pltpu.SemaphoreType.DMA((steps,))],
        compiler_params=pltpu.CompilerParams(vmem_limit_bytes=24 * MIB, dimension_semantics=("arbitrary",)),
        name="unpack",
    )(*extra_smem, *inputs)


def regroup(wire):
    return lax.all_to_all(wire, "comp", split_axis=0, concat_axis=0, tiled=True)


def on_device(spectrum, mask, depth_level, speed_table, wind_u, wind_v, substeps, coupling):
    per_group, rows, columns = spectrum.shape
    group_index = lax.axis_index("comp")
    tiles = rows // SUBS
    edges = jnp.concatenate([spectrum[:, :2], spectrum[:, -2:]], axis=1) * jnp.concatenate([mask[:2], mask[-2:]], axis=0).astype(jnp.float32)[None]
    edges = edge_rows(edges, "space", 2)
    spot = jnp.stack([group_index % SUBS, group_index // SUBS])
    guests = [tiles // 2 - 1, tiles // 2]
    hosts = [t for t in range(tiles) if t not in guests]

    def step(hosts, guests, filling, east, north, turns, back):
        layout = Layout(rows, columns, hosts, guests)
        wire = Wire(layout, per_group, range(len(hosts)))
        values = regroup(propagate(layout, wire, spectrum, edges, mask, depth_level, speed_table, group_index, filling))
        values = regroup(apply_source(wire, values, per_group, spot, east, north, turns, coupling))
        return unpack(layout, [wire], [values], per_group, mask, back)

    fill, spare, back, east, north, turns, flag, back_flag, fits = make_plan(
        Layout(rows, columns, hosts, guests), mask, wind_u, wind_v, substeps
    )
    every = jnp.broadcast_to(substeps.astype(jnp.float32)[:, None], mask.shape)
    return lax.cond(
        fits[0] > 0,
        lambda: step(hosts, guests, (fill, spare, flag), east, north, turns, (back, back_flag)),
        lambda: step(list(range(tiles)), [], None, wind_u, wind_v, every, None),
    )


def solution(mesh):
    placed = (
        P("comp", "space", None),
        P("space", None),
        P("space", None),
        P(),
        P("space", None),
        P("space", None),
        P("space"),
        P(),
    )
    return jax.shard_map(
        on_device, mesh=mesh, in_specs=placed, out_specs=P("comp", "space", None), check_vma=False
    )
```

```python
import math

import jax
import jax.numpy as jnp
import numpy as np
from jax import lax
from jax.experimental import pallas as pl
from jax.experimental.pallas import tpu as pltpu
from jax.sharding import PartitionSpec as P

NF = 36
ND = 36
LEVELS = 8

TIME_STEP = 1.0
WIND_RATE = 0.3
BREAK_RATE = 0.8
MIXING = 0.5

LANES = 128
SUBS = 8
MIB = 1024 * 1024


def edge_rows(cells, axis, width):
    count = lax.axis_size(axis)
    ends = count - 1
    head = cells[:, :width]
    tail = cells[:, -width:]
    below = lax.ppermute(tail, axis, [(i, i + 1) for i in range(ends)])
    above = lax.ppermute(head, axis, [(i + 1, i) for i in range(ends)])
    return below, above


def spectral_tables(period):
    frequency = np.arange(NF, dtype=np.float64)
    angle = 2.0 * math.pi / ND * (np.arange(ND) + 0.5)
    norm_total = ND * np.sum(np.power(1.1, 2.0 * frequency))
    phase = WIND_RATE * 1.5 * np.power(1.1, -frequency)
    weight = np.power(1.1, 2.0 * frequency) / norm_total
    damping = BREAK_RATE * (frequency + 1.0) / NF
    by_direction = np.zeros((period, SUBS))
    by_direction[:, 0] = WIND_RATE * np.tile(np.cos(angle), period // ND)
    by_direction[:, 1] = WIND_RATE * np.tile(np.sin(angle), period // ND)
    return phase, weight, damping, jnp.asarray(by_direction.astype(np.float32))


def take_lanes(values, index):
    return jnp.take_along_axis(values, index, axis=1, mode="promise_in_bounds")


class Layout:
    def __init__(self, rows, columns, hosts, guests):
        self.tiles = rows // SUBS
        self.halves = columns // LANES
        self.hosts = hosts
        self.guest_tiles = guests
        self.guests = [(t, h) for t in guests for h in range(self.halves)]
        self.blocks = [(i, h) for i in range(len(hosts)) for h in range(self.halves)]
        self.share = len(hosts) // len(guests) if guests else 0

    def guest_of(self, i, h):
        return (i // self.share) * self.halves + h


def view(ref, t, h):
    return ref[pl.ds(t * SUBS, SUBS), pl.ds(h * LANES, LANES)]


def count_blocks(layout, mask_ref):
    marked = [1 - view(mask_ref, layout.hosts[i], h) for i, h in layout.blocks]
    marked = jnp.concatenate(marked + [view(mask_ref, t, h) for t, h in layout.guests], axis=0)
    lane = lax.broadcasted_iota(jnp.int32, marked.shape, 1)
    upto = (lax.broadcasted_iota(jnp.int32, (LANES, LANES), 0) <= lax.broadcasted_iota(jnp.int32, (LANES, LANES), 1)).astype(jnp.bfloat16)
    total = jnp.dot(marked.astype(jnp.bfloat16), upto, preferred_element_type=jnp.float32).astype(jnp.int32)
    rank = total - marked
    state = jnp.where(marked > 0, lane + LANES * (lane - rank), -1)
    for bit in range(7):
        moved = pltpu.roll(state, LANES - (1 << bit), 1)
        take = (moved >= 0) & (((moved >> (7 + bit)) & 1) == 1)
        stay = (state >= 0) & (((state >> (7 + bit)) & 1) == 0)
        state = jnp.where(take, moved, jnp.where(stay, state, -1))
    place = jnp.maximum(state, 0) & (LANES - 1)
    count = jnp.broadcast_to(total[:, LANES - 1:], marked.shape)

    def parts(array):
        each = [array[i:i + SUBS] for i in range(0, array.shape[0], SUBS)]
        return each[:len(layout.blocks)], each[len(layout.blocks):]

    return parts(marked), parts(rank), parts(place), parts(count)


class Plan:
    def __init__(self, layout, mask_ref):
        (hole, self.sea), (self.hole_rank, self.sea_rank), (self.hole_at, self.sea_at), counts = count_blocks(layout, mask_ref)
        self.hole_count, self.sea_count = counts
        self.hole = [m > 0 for m in hole]
        self.sea = [m > 0 for m in self.sea]
        guests = len(layout.guests)
        zero = jnp.zeros((SUBS, LANES), jnp.int32)
        self.start = []
        self.holes_of = [zero] * guests
        for b, at in enumerate(layout.blocks):
            j = layout.guest_of(*at)
            self.start.append(self.holes_of[j])
            self.holes_of[j] = self.holes_of[j] + self.hole_count[b]
        self.open_of = [jnp.maximum(self.holes_of[j] - self.sea_count[j], 0) for j in range(guests)]
        self.left_of = [jnp.maximum(self.sea_count[j] - self.holes_of[j], 0) for j in range(guests)]
        self.open_start, self.left_start = [zero], [zero]
        for j in range(1, guests):
            self.open_start.append(self.open_start[-1] + self.open_of[j - 1])
            self.left_start.append(self.left_start[-1] + self.left_of[j - 1])


def inside(index):
    return jnp.clip(index, 0, LANES - 1)


VMEM_SPEC = pl.BlockSpec(memory_space=pltpu.VMEM)
SMEM_SPEC = pl.BlockSpec(memory_space=pltpu.SMEM)


def make_plan(layout, mask, wind_u, wind_v, substeps):
    columns = mask.shape[1]

    def body(mask_ref, u_ref, v_ref, n_ref, fill_ref, spare_ref, back_ref, uo_ref, vo_ref, no_ref, flag_ref, back_flag, fits_ref):
        p = Plan(layout, mask_ref)
        subrow = lax.broadcasted_iota(jnp.int32, (SUBS, LANES), 0)
        ranks = []

        def turns_of(t):
            result = jnp.zeros((SUBS, LANES), jnp.int32)
            for r in range(SUBS):
                result = jnp.where(subrow == r, n_ref[t * SUBS + r], result)
            return result.astype(jnp.float32)

        every = {t: turns_of(t) for t in range(layout.tiles)}
        for b, (i, h) in enumerate(layout.blocks):
            own = layout.guest_of(i, h)
            rank = p.start[b] + p.hole_rank[b]
            ranks.append(rank)
            first = take_lanes(p.sea_at[own], inside(rank))
            place = (pl.ds(i * SUBS, SUBS), pl.ds(h * LANES, LANES))
            fill_ref[place] = first
            flag_ref[b] = -1
            hole = p.hole[b]
            for source, target in ((u_ref, uo_ref), (v_ref, vo_ref)):
                value = take_lanes(view(source, *layout.guests[own]), first)
                target[place] = jnp.where(hole, value, view(source, layout.hosts[i], h))
            guest = jnp.where(rank < p.sea_count[own], every[layout.guests[own][0]], 1.0)
            no_ref[place] = jnp.where(hole, guest, every[layout.hosts[i]])

        for j, (t, h) in enumerate(layout.guests):
            rank = p.sea_rank[j]
            back = jnp.full((SUBS, LANES), -1, jnp.int32)
            for b, block in enumerate(layout.blocks):
                if layout.guest_of(*block) == j:
                    ok = p.sea[j] & (rank >= p.start[b]) & (rank < p.start[b] + p.hole_count[b])
                    back = jnp.where(ok, LANES * b + take_lanes(p.hole_at[b], inside(rank - p.start[b])), back)
            back_ref[pl.ds(layout.guest_tiles.index(t) * SUBS, SUBS), pl.ds(h * LANES, LANES)] = back
            back_flag[j] = 0

        left = sum(p.left_of)
        flag_ref[len(layout.blocks)] = jnp.max(left)
        fits_ref[0] = (jnp.max(left - sum(p.open_of)) <= 0).astype(jnp.int32)

        @pl.when(jnp.max(left) > 0)
        def _():
            spare_ref[...] = jnp.full(spare_ref.shape, -1, jnp.int32)
            for j, guest in enumerate(layout.guests):
                @pl.when(jnp.max(p.left_of[j]) > 0)
                def _():
                    for b, (i, h) in enumerate(layout.blocks):
                        own = layout.guest_of(i, h)
                        if own == j:
                            continue
                        extra = p.open_start[own] + ranks[b] - p.sea_count[own] - p.left_start[j]
                        ok = p.hole[b] & (ranks[b] >= p.sea_count[own]) & (extra >= 0) & (extra < p.left_of[j])
                        found = take_lanes(p.sea_at[j], inside(extra + p.holes_of[j]))
                        place = (pl.ds(i * SUBS, SUBS), pl.ds(h * LANES, LANES))
                        spare_ref[place] = jnp.where(ok, LANES * j + found, spare_ref[place])
                        for source, target in ((u_ref, uo_ref), (v_ref, vo_ref)):
                            target[place] = jnp.where(ok, take_lanes(view(source, *guest), found), target[place])
                        no_ref[place] = jnp.where(ok, every[guest[0]], no_ref[place])
            for b, (i, h) in enumerate(layout.blocks):
                flag_ref[b] = jnp.max(view(spare_ref, i, h))

            for j, (t, h) in enumerate(layout.guests):
                @pl.when(jnp.max(p.left_of[j]) > 0)
                def _():
                    place = (pl.ds(layout.guest_tiles.index(t) * SUBS, SUBS), pl.ds(h * LANES, LANES))
                    back = back_ref[place]
                    rank = p.sea_rank[j]
                    extra = p.left_start[j] + rank - p.holes_of[j]
                    for b, block in enumerate(layout.blocks):
                        own = layout.guest_of(*block)
                        if own != j:
                            at = extra - p.open_start[own] + p.sea_count[own]
                            ok = p.sea[j] & (rank >= p.holes_of[j])
                            ok = ok & (extra >= p.open_start[own]) & (extra < p.open_start[own] + p.open_of[own])
                            ok = ok & (at >= p.start[b]) & (at < p.start[b] + p.hole_count[b])
                            back = jnp.where(ok, LANES * b + take_lanes(p.hole_at[b], inside(at - p.start[b])), back)
                    back_ref[place] = back
                    back_flag[j] = 1

    whole = (len(layout.hosts) * SUBS, columns)
    return pl.pallas_call(
        body,
        in_specs=[VMEM_SPEC] * 3 + [SMEM_SPEC],
        out_specs=[VMEM_SPEC] * 6 + [SMEM_SPEC] * 3,
        out_shape=[
            jax.ShapeDtypeStruct(whole, jnp.int32),
            jax.ShapeDtypeStruct(whole, jnp.int32),
            jax.ShapeDtypeStruct((len(layout.guest_tiles) * SUBS, columns), jnp.int32),
            jax.ShapeDtypeStruct(whole, jnp.float32),
            jax.ShapeDtypeStruct(whole, jnp.float32),
            jax.ShapeDtypeStruct(whole, jnp.float32),
            jax.ShapeDtypeStruct((len(layout.blocks) + 1,), jnp.int32),
            jax.ShapeDtypeStruct((len(layout.guests),), jnp.int32),
            jax.ShapeDtypeStruct((1,), jnp.int32),
        ],
        name="plan",
    )(mask, wind_u, wind_v, substeps)


class Wire:
    def __init__(self, layout, per_group, tiles):
        self.tiles = tiles
        self.even = per_group // SUBS * SUBS
        self.rest = per_group - self.even
        self.rest_start = len(tiles) * self.even
        self.pitch = -(-(len(tiles) * per_group) // SUBS) * SUBS
        self.groups = SUBS * layout.halves
        self.blocks = [b for b, (i, h) in enumerate(layout.blocks) if i in tiles]

    def row(self, t, c):
        t = t - self.tiles[0]
        return jnp.where(c < self.even, t * self.even + c, self.rest_start + t * self.rest + c - self.even)

    def lines(self, t, h, c):
        return pl.ds(h * SUBS * self.pitch + self.row(t, c), SUBS, stride=self.pitch)


def propagate(layout, wire, spectrum, edges, mask, depth_level, speed_table, group_index, filling):
    per_group, rows, columns = spectrum.shape
    run = ND // 4
    steps = per_group // run
    angle = 2.0 * math.pi / ND * (np.arange(ND) + 0.5)
    turns = jnp.asarray(np.abs(np.stack([np.cos(angle), np.sin(angle)])).astype(np.float32))
    packed = len(layout.guests) > 0
    tiles = sorted([layout.hosts[i] for i in wire.tiles] + layout.guest_tiles)
    edged = len(edges) > 0

    def body(*refs):
        refs = list(refs)
        first_ref, turn_ref, speed_ref = refs[:3]
        flag_ref, left_ref = refs[3:5] if packed else (None, None)
        refs = refs[3 + 2 * packed:]
        spec_ref = refs[0]
        below_ref, above_ref = refs[1:3] if edged else (None, None)
        refs = refs[1 + 2 * edged:]
        mask_ref, depth_ref = refs[:2]
        fill_ref, spare_ref = refs[2:4] if packed else (None, None)
        out_ref, base_ref, sea_ref, pad_ref, field_ref, one_ref, two_ref = refs[2 + 2 * packed:]
        step = pl.program_id(0)
        start = first_ref[0] + step * run
        f = start // ND

        @pl.when(step == 0)
        def _():
            sea_ref[...] = mask_ref[...].astype(jnp.float32)

        @pl.when((step == 0) | (start % ND == 0))
        def _():
            for t in tiles:
                place = pl.ds(t * SUBS, SUBS)
                level = depth_ref[place, :]
                speed = jnp.zeros(level.shape, jnp.float32)
                for l in range(LEVELS):
                    speed = jnp.where(level == l, speed_ref[l, f], speed)
                base_ref[place, :] = speed

        lane = lax.broadcasted_iota(jnp.int32, (SUBS, LANES), 1)

        def sweep(centre, near, far, one, two):
            return centre + one * (near - centre) + two * (far - centre)

        def factors(cc, carry):
            wide = turn_ref[0, start % ND + cc]
            for t in tiles:
                place = pl.ds(t * SUBS, SUBS)
                amount = base_ref[place, :] * wide
                one = amount * (2.0 - amount)
                one_ref[cc, place, :] = one
                two_ref[cc, place, :] = 0.5 * (amount - one)
            return carry

        lax.fori_loop(0, run, factors, 0, unroll=3)

        def shifted(parts, by):
            turned = [pltpu.roll(part, by % LANES, 1) for part in parts]
            edge = jnp.zeros_like(turned[0])
            if by > 0:
                return [jnp.where(lane >= by, turned[i], turned[i - 1] if i else edge) for i in range(len(parts))]
            ends = turned[1:] + [edge]
            return [jnp.where(lane < LANES + by, turned[i], ends[i]) for i in range(len(parts))]

        def run_all(sign_x, sign_y):
            def component(cc, carry):
                needed = sorted({n for t in tiles for n in (t, t - sign_x) if 0 <= n < layout.tiles})
                if edged:
                    pad_ref[cc, pl.ds(SUBS - 2, 2), :] = below_ref[step * run + cc]
                    pad_ref[cc, pl.ds(rows + SUBS, 2), :] = above_ref[step * run + cc]
                for t in needed:
                    place = pl.ds(t * SUBS, SUBS)
                    pad_ref[cc, pl.ds((t + 1) * SUBS, SUBS), :] = spec_ref[cc, place, :] * sea_ref[place, :]
                for t in tiles:
                    place = pl.ds(t * SUBS, SUBS)
                    at = (t + 1) * SUBS
                    centre = pad_ref[cc, pl.ds(at, SUBS), :]
                    near = pad_ref[cc, pl.ds(at - sign_x, SUBS), :]
                    far = pad_ref[cc, pl.ds(at - 2 * sign_x, SUBS), :]
                    centre = sweep(centre, near, far, one_ref[cc, place, :], two_ref[cc, place, :]) * sea_ref[place, :]
                    parts = [centre[:, h * LANES:(h + 1) * LANES] for h in range(layout.halves)]
                    near = shifted(parts, sign_y)
                    far = shifted(parts, 2 * sign_y)
                    for h in range(layout.halves):
                        lanes = slice(h * LANES, (h + 1) * LANES)
                        one, two = one_ref[run - 1 - cc, place, lanes], two_ref[run - 1 - cc, place, lanes]
                        field_ref[cc, place, lanes] = sweep(parts[h], near[h], far[h], one, two)
                return carry

            lax.fori_loop(0, run, component, 0, unroll=9)

        quadrant = (start % ND) // run
        for at, signs in enumerate(((1, 1), (-1, 1), (-1, -1), (1, -1))):
            pl.when(quadrant == at)(lambda signs=signs: run_all(*signs))

        def put(t, h, cc, value):
            out_ref[wire.lines(t, h, step * run + cc), :] = value

        def base_value(t, h, cc):
            value = view(field_ref.at[cc], layout.hosts[t], h)
            if packed:
                guest = view(field_ref.at[cc], *layout.guests[layout.guest_of(t, h)])
                value = jnp.where(view(sea_ref, layout.hosts[t], h) > 0.0, value, take_lanes(guest, view(fill_ref, t, h)))
            return value

        for b in wire.blocks:
            for cc in range(run):
                put(*layout.blocks[b], cc, base_value(*layout.blocks[b], cc))
        if not packed:
            return

        def fill_spare(b, j):
            t, h = layout.blocks[b]
            spare = view(spare_ref, t, h)
            for cc in range(run):
                lines = wire.lines(t, h, step * run + cc)
                other = take_lanes(view(field_ref.at[cc], *layout.guests[j]), spare & (LANES - 1))
                out_ref[lines, :] = jnp.where(spare >> 7 == j, other, out_ref[lines, :])

        @pl.when(flag_ref[len(layout.blocks)] > 0)
        def _():
            for b in wire.blocks:
                for j in range(len(layout.guests)):
                    if j != layout.guest_of(*layout.blocks[b]):
                        pl.when((flag_ref[b] >= 0) & (left_ref[j] != 0))(lambda b=b, j=j: fill_spare(b, j))

    smem = pl.BlockSpec(memory_space=pltpu.SMEM)

    extra_smem = list(filling[2:]) if packed else []
    extra = list(filling[:2]) if packed else []
    shape = (wire.groups * wire.pitch, LANES)
    out = pl.pallas_call(
        body,
        grid=(steps,),
        in_specs=[smem] * (3 + len(extra_smem)) + [pl.BlockSpec((run, rows, columns), lambda i: (i, 0, 0))] + [VMEM_SPEC] * (len(edges) + 2 + len(extra)),
        out_specs=VMEM_SPEC,
        out_shape=jax.ShapeDtypeStruct(shape, jnp.float32),
        scratch_shapes=[
            pltpu.VMEM((rows, columns), jnp.float32),
            pltpu.VMEM((rows, columns), jnp.float32),
            pltpu.VMEM((run, rows + 2 * SUBS, columns), jnp.float32),
            pltpu.VMEM((run, rows, columns), jnp.float32),
            pltpu.VMEM((run, rows, columns), jnp.float32),
            pltpu.VMEM((run, rows, columns), jnp.float32),
        ],
        compiler_params=pltpu.CompilerParams(vmem_limit_bytes=24 * MIB, dimension_semantics=("arbitrary",)),
        name="propagate",
    )((group_index * per_group).reshape(1), turns, speed_table.T, *extra_smem, spectrum, *edges, mask, depth_level, *extra)
    return out.reshape(wire.groups, wire.pitch, LANES)


def apply_source(wire, values, per_group, spot, east, north, turns, coupling):
    groups, pitch, even = wire.groups, wire.pitch, wire.even
    total = groups * per_group
    pairs = len(wire.tiles) // 2
    period = 2 * ND
    pieces = 9
    piece = total // pieces
    phase, weight, damping, by_direction = spectral_tables(period)

    def body(spot_ref, wire_ref, east_ref, north_ref, turn_ref, coupling_ref, dir_ref, out_ref,
             low_ref, high_ref, round_ref, wind_ref, mix_ref, rest_ref):
        pair = pl.program_id(0)
        value_refs = (low_ref, high_ref)
        subrow = lax.broadcasted_iota(jnp.int32, (SUBS, LANES), 0)

        def constant(table, start):
            low, high = start // ND, (start + SUBS - 1) // ND
            if low == high:
                return float(table[low])
            return jnp.where(subrow < high * ND - start, float(table[low]), float(table[high]))

        def line(ref, half):
            tile = ref[pl.ds(pl.multiple_of((2 * pair + half) * SUBS, SUBS), SUBS), :]
            tile = jnp.where(spot_ref[1] == 0, tile[:, :LANES], tile[:, LANES:])
            row = jnp.sum(jnp.where(subrow == spot_ref[0], tile, 0.0), axis=0, keepdims=True)
            return jnp.broadcast_to(row, (SUBS, LANES))

        @pl.when(pair == 0)
        def _():
            for k in range(groups):
                rest_ref[pl.ds(k * SUBS, SUBS), :] = wire_ref[k, pl.ds(pitch - SUBS, SUBS), :]

        def rows_of(half):
            return pl.ds(pl.multiple_of((2 * pair + half) * even, SUBS), even)

        turn_line = [line(turn_ref, half) for half in range(2)]
        step_line = [TIME_STEP / t for t in turn_line]
        for half, ref in enumerate(value_refs):
            for k in range(groups):
                ref[pl.ds(k * per_group, even), :] = wire_ref[k, rows_of(half), :]
            ref[pl.ds(even, groups, stride=per_group), :] = rest_ref[pl.ds(2 * pair + half, groups, stride=SUBS), :]
            east_line, north_line = line(east_ref, half), line(north_ref, half)
            for i in range(0, period, SUBS):
                columns = dir_ref[pl.ds(i, SUBS), :]
                wind_ref[pl.ds(i, SUBS), pl.ds(half * LANES, LANES)] = east_line * columns[:, 0:1] + north_line * columns[:, 1:2]

        def sweep(change):
            squares = []
            for half, ref in enumerate(value_refs):
                steep = jnp.zeros((SUBS, LANES), jnp.float32)
                for f in range(0, NF, 2):
                    sums = [None, None]
                    for start in range(f * ND, (f + 2) * ND, SUBS):
                        place = pl.ds(start, SUBS)
                        value = ref[place, :]
                        if change is not None:
                            value = change(half, start, value)
                            ref[place, :] = value
                        low, high = start // ND, (start + SUBS - 1) // ND
                        if low != high:
                            steep = steep + constant(weight, start) * value
                        else:
                            sums[low - f] = value if sums[low - f] is None else sums[low - f] + value
                    steep = steep + float(weight[f]) * sums[0] + float(weight[f + 1]) * sums[1]
                steepness = jnp.broadcast_to(jnp.sum(steep, axis=0, keepdims=True), (SUBS, LANES))
                squares.append(steepness * steepness)
            return tuple(squares)

        def round_all():
            for half, ref in enumerate(value_refs):
                for start in range(0, total, 2 * SUBS):
                    place = pl.ds(start, 2 * SUBS)
                    round_ref[place, pl.ds(half * LANES, LANES)] = ref[place, :].astype(jnp.bfloat16)

        def turn(repeat, squares):
            for i in range(pieces):
                place = pl.ds(i * piece, piece)
                mix_ref[place, :] = jnp.dot(coupling_ref[place, :], round_ref[...], preferred_element_type=jnp.float32)

            def change(half, start, value):
                lanes = pl.ds(half * LANES, LANES)
                rate = jnp.maximum(0.0, wind_ref[pl.ds(start % period, SUBS), lanes] - constant(phase, start))
                rate = rate - constant(damping, start) * squares[half]
                step = step_line[half]
                moved = value + step * (rate * value + MIXING * mix_ref[pl.ds(start, SUBS), lanes])
                return jnp.where(repeat.astype(jnp.float32) < turn_line[half], moved, value)

            squares = sweep(change)
            round_all()
            return squares

        squares = sweep(None)
        round_all()
        most = jnp.max(jnp.maximum(turn_line[0], turn_line[1])).astype(jnp.int32)
        lax.fori_loop(0, most, turn, squares)

        for half, ref in enumerate(value_refs):
            for k in range(groups):
                out_ref[k, rows_of(half), :] = ref[pl.ds(k * per_group, even), :]
            rest_ref[pl.ds(2 * pair + half, groups, stride=SUBS), :] = ref[pl.ds(even, groups, stride=per_group), :]

        @pl.when(pair == pairs - 1)
        def _():
            for k in range(groups):
                out_ref[k, pl.ds(pitch - SUBS, SUBS), :] = rest_ref[pl.ds(k * SUBS, SUBS), :]

    return pl.pallas_call(
        body,
        grid=(pairs,),
        in_specs=[SMEM_SPEC] + [VMEM_SPEC] * 6,
        out_specs=VMEM_SPEC,
        out_shape=jax.ShapeDtypeStruct((groups, pitch, LANES), jnp.float32),
        scratch_shapes=[
            pltpu.VMEM((total, LANES), jnp.float32),
            pltpu.VMEM((total, LANES), jnp.float32),
            pltpu.VMEM((total, 2 * LANES), jnp.bfloat16),
            pltpu.VMEM((period, 2 * LANES), jnp.float32),
            pltpu.VMEM((total, 2 * LANES), jnp.float32),
            pltpu.VMEM((groups * SUBS, LANES), jnp.float32),
        ],
        compiler_params=pltpu.CompilerParams(vmem_limit_bytes=32 * MIB, dimension_semantics=("arbitrary",)),
        name="source",
    )(spot, values, east, north, turns, coupling, by_direction)


def unpack(layout, wires, arrays, per_group, mask, back):
    run = ND // 4
    steps = per_group // run
    rows, columns = mask.shape
    packed = len(layout.guests) > 0

    def body(*refs):
        refs = list(refs)
        flag_ref = refs.pop(0) if packed else None
        spare_flag = refs.pop(0) if packed else None
        wire_refs = [refs.pop(0) for _ in wires]
        mask_ref = refs.pop(0)
        back_ref = refs.pop(0) if packed else None
        target_ref, held_ref, sem = refs
        step = pl.program_id(0)
        out_ref = held_ref.at[pl.ds(step * run, run)]

        def get(t, h, cc):
            for wire, ref in zip(wires, wire_refs):
                if t in wire.tiles:
                    return ref[wire.lines(t, h, step * run + cc), :]

        def fetch(j, blocks):
            t, h = layout.guests[j]
            place = (pl.ds(t * SUBS, SUBS), pl.ds(h * LANES, LANES))
            back = view(back_ref, layout.guest_tiles.index(t), h)
            for cc in range(run):
                value = jnp.zeros((SUBS, LANES), jnp.float32)
                for b in blocks:
                    found = take_lanes(get(*layout.blocks[b], cc), back & (LANES - 1))
                    value = jnp.where(back >> 7 == b, found, value)
                out_ref[(cc,) + place] = value

        def fetch_spare(j, b):
            t, h = layout.guests[j]
            place = (pl.ds(t * SUBS, SUBS), pl.ds(h * LANES, LANES))
            back = view(back_ref, layout.guest_tiles.index(t), h)
            for cc in range(run):
                found = take_lanes(get(*layout.blocks[b], cc), back & (LANES - 1))
                out_ref[(cc,) + place] = jnp.where(back >> 7 == b, found, out_ref[(cc,) + place])

        for i, h in layout.blocks:
            place = (pl.ds(layout.hosts[i] * SUBS, SUBS), pl.ds(h * LANES, LANES))
            sea = mask_ref[place] > 0
            for cc in range(run):
                out_ref[(cc,) + place] = jnp.where(sea, get(i, h, cc), 0.0)
        for j in range(len(layout.guests)):
            fetch(j, [b for b, at in enumerate(layout.blocks) if layout.guest_of(*at) == j])
        for j in range(len(layout.guests)):
            @pl.when(flag_ref[j] != 0)
            def _():
                for b, at in enumerate(layout.blocks):
                    if layout.guest_of(*at) != j:
                        pl.when(spare_flag[b] >= 0)(lambda b=b: fetch_spare(j, b))

        def send(at):
            place = pl.ds(at * run, run)
            return pltpu.make_async_copy(held_ref.at[place], target_ref.at[place], sem.at[at])

        send(step).start()

        @pl.when(step == steps - 1)
        def _():
            for at in range(steps):
                send(at).wait()

    smem = pl.BlockSpec(memory_space=pltpu.SMEM)
    extra_smem = list(back[1:]) if packed else []
    inputs = [array.reshape(-1, LANES) for array in arrays] + [mask] + ([back[0]] if packed else [])
    return pl.pallas_call(
        body,
        grid=(steps,),
        in_specs=[smem] * len(extra_smem) + [VMEM_SPEC] * len(inputs),
        out_specs=pl.BlockSpec(memory_space=pltpu.HBM),
        out_shape=pltpu.HBM((per_group, rows, columns), jnp.float32),
        scratch_shapes=[pltpu.VMEM((per_group, rows, columns), jnp.float32), pltpu.SemaphoreType.DMA((steps,))],
        compiler_params=pltpu.CompilerParams(vmem_limit_bytes=24 * MIB, dimension_semantics=("arbitrary",)),
        name="unpack",
    )(*extra_smem, *inputs)


def regroup(wire):
    return lax.all_to_all(wire, "comp", split_axis=0, concat_axis=0, tiled=True)


def on_device(spectrum, mask, depth_level, speed_table, wind_u, wind_v, substeps, coupling):
    per_group, rows, columns = spectrum.shape
    group_index = lax.axis_index("comp")
    tiles = rows // SUBS
    edges = jnp.concatenate([spectrum[:, :2], spectrum[:, -2:]], axis=1) * jnp.concatenate([mask[:2], mask[-2:]], axis=0).astype(jnp.float32)[None]
    edges = edge_rows(edges, "space", 2)
    spot = jnp.stack([group_index % SUBS, group_index // SUBS])
    guests = [tiles // 2 - 1, tiles // 2]
    hosts = [t for t in range(tiles) if t not in guests]

    def step(hosts, guests, filling, east, north, turns, back):
        layout = Layout(rows, columns, hosts, guests)
        wire = Wire(layout, per_group, range(len(hosts)))
        values = regroup(propagate(layout, wire, spectrum, edges, mask, depth_level, speed_table, group_index, filling))
        values = regroup(apply_source(wire, values, per_group, spot, east, north, turns, coupling))
        return unpack(layout, [wire], [values], per_group, mask, back)

    fill, spare, back, east, north, turns, flag, back_flag, fits = make_plan(
        Layout(rows, columns, hosts, guests), mask, wind_u, wind_v, substeps
    )
    every = jnp.broadcast_to(substeps.astype(jnp.float32)[:, None], mask.shape)
    return lax.cond(
        fits[0] > 0,
        lambda: step(hosts, guests, (fill, spare, flag, back_flag), east, north, turns, (back, back_flag, flag)),
        lambda: step(list(range(tiles)), [], None, wind_u, wind_v, every, None),
    )


def solution(mesh):
    placed = (
        P("comp", "space", None),
        P("space", None),
        P("space", None),
        P(),
        P("space", None),
        P("space", None),
        P("space"),
        P(),
    )
    return jax.shard_map(
        on_device, mesh=mesh, in_specs=placed, out_specs=P("comp", "space", None), check_vma=False
    )
```
